256 devices in a mesh: dp: 8 (over y, x_lo), expert: 32 (over x_hi, z, core).
Axes of the slice: x: 4 (x_hi: 2, x_lo: 2; x = x_hi * 2 + x_lo), y: 4, z: 8, core: 2. Of those that a mesh axis runs over, the one named last changes fastest.
Arguments:
- tokens: bfloat16 [32, 8, 12, 7168], P('expert', 'dp'), may hold values from -6 to 6
- cotangent: bfloat16 [32, 8, 12, 7168], P('expert', 'dp'), may hold values from -6 to 6
- w_gate: bfloat16 [32, 7168, 1024], P('expert', None, 'dp'), may hold values from -0.0625 to 0.0625
- w_up: bfloat16 [32, 7168, 1024], P('expert', None, 'dp'), may hold values from -0.0625 to 0.0625
- w_down: bfloat16 [32, 1024, 7168], P('expert', 'dp'), may hold values from -0.1875 to 0.1875
- routes: int32 [32, 8, 12, 2], P('expert', 'dp'), may hold values from 0 to 31, all different within a row; in each aligned block of 96 rows (0 to 95, 96 to 191, ..., all dimensions but the last counted through in order) at most 9 rows name the same one
- gates: int32 [32, 8, 12, 2], P('expert', 'dp'), may hold values from 4096 to 65535
- matching: int32 [32], replicated, may hold values from 0 to 31, as said below
Outputs:
- grad_input: bfloat16 [32, 8, 12, 7168], P('expert', 'dp')
- grad_gate: bfloat16 [32, 7168, 1024], P('expert', None, 'dp')
- grad_up: bfloat16 [32, 7168, 1024], P('expert', None, 'dp')
- grad_down: bfloat16 [32, 1024, 7168], P('expert', 'dp')
The draws below stay inside these ranges and needn't reach their ends.
Inputs may be any that keep to these rules, and one draw needn't show every extreme that they name: Each token names 2 different experts. Within routes[c] for any c no expert is named more than 9 times. matching[j] is j, or j + 16 for j below 16, or j - 16 above; matching[matching[j]] = j, and the pair of slot 31 always differs from it.
All inputs are finite; a program needn't handle non-finite values.
Results may differ from the reference program's by a relative error of at most 0.019.
Values may be sent and summed in bfloat16 or wider, within the bound.
No kernel may reach another device: no remote copies, remote signals or barrier semaphores. Data moves between devices by JAX's collectives and lax.ppermute only.
A program may use at most 192 MiB of HBM per device.

```python
import math
import jax
import jax.numpy as jnp
import numpy as np
from jax import lax

D = 7168
FF = 1024
TOPK = 2
TOK_DEV = 12
EXPERTS = 32
HIDDEN_DEV = 128
CAPC = 9
N_DP = 8


def draw_matching(key, part):
    half = EXPERTS // 2
    flags = jax.random.randint(key, (half,), 0, 2)
    lower = jnp.arange(half, dtype=jnp.int32)
    flags = jnp.where(lower == half - 1, 1, flags).astype(jnp.int32)
    first = lower + flags * half
    second = lower + half - flags * half
    return jnp.concatenate([first, second]).astype(jnp.int32)


def place_ends(entries, key, smallest, high):
    longest = entries.shape.index(max(entries.shape))
    spots = []
    for shift in (0, 1):
        where = [jax.random.randint(jax.random.fold_in(key, axis), (), 0, length) for axis, length in enumerate(entries.shape)]
        where[longest] = (where[longest] + shift) % entries.shape[longest]
        spots.append(tuple(where))
    return entries.at[spots[0]].set(smallest).at[spots[1]].set(high)


def shard_levels(key, shape, split, least, largest):
    factor_of, own = 1.0, jax.random.fold_in(key, 6)
    for axis_at, parts in split:
        steps = jnp.exp(jax.random.uniform(jax.random.fold_in(own, axis_at), (parts,), jnp.float32, least / len(split), largest / len(split)))
        factor_of = factor_of * jnp.repeat(steps, shape[axis_at] // parts).reshape([-1 if axis == axis_at else 1 for axis in range(len(shape))])
    return factor_of


def routed_block(own_key, own, number, rows, count, top, limit, lean):
    sequence = jax.random.permutation(own_key, count)
    heavy_load, usual = portions_of(count, rows * top, limit, lean, True), portions_of(count, rows * top, limit, lean, False)
    places = jnp.arange(count)

    def named(tallies, turn):
        used = int((tallies > 0).sum())
        fixed = max(1, used // 4)
        moved = fixed + (places - fixed + turn * (used - fixed)) % max(1, count - fixed)
        return jnp.zeros((count,), jnp.int32).at[sequence[jnp.where(places < fixed, places, moved)]].set(jnp.asarray(tallies, jnp.int32))

    tallies = jnp.where(number % 4 == 0, named(heavy_load, number // 4), named(usual, number - number // 4 - 1))
    mixed = jax.random.permutation(jax.random.fold_in(own, 3), count)
    donor, receiver = mixed[0:count // 2 * 2:2], mixed[1:count // 2 * 2:2]
    margin = jnp.minimum(tallies[donor] - 1, limit - tallies[receiver]) // 2
    margin = jnp.where((donor == sequence[0]) | (receiver == sequence[0]) | (tallies[receiver] == 0), 0, jnp.maximum(margin, 0))
    moved = jax.random.randint(jax.random.fold_in(own, 4), (count // 2,), 0, 1 << 20) % (margin + 1)
    tallies = tallies.at[donor].add(-moved).at[receiver].add(moved)
    items = jnp.searchsorted(jnp.cumsum(tallies), jnp.arange(rows * top), side="right").astype(jnp.int32)
    grid = items.reshape(top, rows).T
    grid = grid[jax.random.permutation(jax.random.fold_in(own, 1), rows)]
    turn = jax.random.randint(jax.random.fold_in(own, 2), (rows, 1), 0, top)
    return jnp.take_along_axis(grid, (jnp.arange(top)[None, :] + turn) % top, axis=1)


def portions_of(number_of, total, most, slope, full):
    weights = [(1 << 20) // math.isqrt(standing ** slope) + 1 for standing in range(1, number_of + 1)]
    largest = most if full else min(most, max(-(-total // number_of), total * weights[0] // sum(weights)))
    least = 1 if total - largest >= number_of - 1 else 0
    given, rest = [largest] + [least] * (number_of - 1), total - largest - least * (number_of - 1)
    while rest > 0:
        candidates = [i for i in range(1, number_of) if given[i] < largest] or [i for i in range(1, number_of) if given[i] < most]
        mass, remaining = sum([weights[i] for i in candidates]), rest
        for i in candidates:
            more = min(most - given[i], max(1, remaining * weights[i] // mass), rest)
            given[i] = given[i] + more
            rest = rest - more
    return np.array(given)


def centred(stream_key, shape, scale, most, cuts=(), kind=jnp.bfloat16):
    values = jax.random.normal(stream_key, shape, jnp.float32) * scale
    if len(cuts) > 0:
        values = shard_levels(stream_key, shape, cuts, -0.22, 0.18) * values
    return jnp.clip(values, min=-most, max=most).astype(kind)


def setup_inputs(seed: int = 0) -> dict:
    arg_keys = jax.random.split(jax.random.key(seed), 9)
    tokens = centred(arg_keys[0], (EXPERTS, N_DP, TOK_DEV, D), 1.0, 6.0, ((0, 32), (1, 8)))
    cotangent = centred(arg_keys[1], (EXPERTS, N_DP, TOK_DEV, D), 1.0, 6.0, ((0, 32), (1, 8)))
    w_gate = centred(arg_keys[2], (EXPERTS, D, FF), D ** -0.5, 0.0625, ((0, 32), (2, 8)))
    w_up = centred(arg_keys[3], (EXPERTS, D, FF), D ** -0.5, 0.0625, ((0, 32), (2, 8)))
    w_down = centred(arg_keys[4], (EXPERTS, FF, D), FF ** -0.5, 0.1875, ((0, 32), (1, 8)))
    routes_keys = jax.random.split(jax.random.fold_in(arg_keys[5], 1), EXPERTS * N_DP * TOK_DEV // (N_DP * TOK_DEV))
    routes_turns = jax.random.permutation(jax.random.fold_in(arg_keys[5], 3), EXPERTS * N_DP * TOK_DEV // (N_DP * TOK_DEV))
    routes = jax.vmap(lambda own, number: routed_block(jax.random.fold_in(arg_keys[5], 2), own, number, N_DP * TOK_DEV, EXPERTS, TOPK, CAPC, 2))(routes_keys, routes_turns).reshape((EXPERTS, N_DP, TOK_DEV, TOPK))
    gates = place_ends(jax.random.randint(arg_keys[6], (EXPERTS, N_DP, TOK_DEV, TOPK), 4096, 65536), jax.random.fold_in(arg_keys[6], 1), 4096, 65535).astype(jnp.int32)
    matching = draw_matching(jax.random.fold_in(arg_keys[8], 71), 0)
    return dict(tokens=tokens, cotangent=cotangent, w_gate=w_gate, w_up=w_up, w_down=w_down, routes=routes, gates=gates, matching=matching)


def reference(tokens, cotangent, w_gate, w_up, w_down, routes, gates, matching):
    width = tokens.shape[-1]
    flat_rows = tokens.reshape(-1, width)
    flat_cot = cotangent.reshape(-1, width)
    choice_ids = routes.reshape(-1).astype(jnp.int32)
    pick_count = choice_ids.shape[0]
    expert_iota = jnp.arange(EXPERTS, dtype=jnp.int32)
    onehot = (choice_ids[:, None] == expert_iota[None, :]).astype(jnp.int32)
    ranking = jnp.sum(jnp.cumsum(onehot, axis=0) * onehot, axis=1) - 1
    table = jnp.full((EXPERTS, EXPERTS * CAPC), pick_count, jnp.int32)
    table = table.at[choice_ids, ranking.astype(jnp.int32)].set(jnp.arange(pick_count, dtype=jnp.int32))
    scale = gates.reshape(-1).astype(jnp.float32) / 65536.0
    groups = FF // HIDDEN_DEV

    def per_expert(total, inputs):
        picked, gate_mat, up_mat, down_mat = inputs
        valid = picked < pick_count
        safe = jnp.minimum(picked, pick_count - 1)
        owner_tok = safe // TOPK
        rows_in = jnp.where(valid[:, None], flat_rows[owner_tok], jnp.zeros((), flat_rows.dtype))
        gated = scale[safe][:, None] * flat_cot[owner_tok].astype(jnp.float32)
        rows_cot = jnp.where(valid[:, None], gated, jnp.zeros((), jnp.float32)).astype(jnp.bfloat16)
        gate_act = jnp.dot(rows_in, gate_mat, preferred_element_type=jnp.float32)
        up_act = jnp.dot(rows_in, up_mat, preferred_element_type=jnp.float32)
        sigmoid_gate = jax.nn.sigmoid(gate_act)
        hidden = (gate_act * sigmoid_gate * up_act).astype(jnp.bfloat16)
        down_grad = jnp.dot(hidden.T, rows_cot, preferred_element_type=jnp.float32)
        d_hidden = jnp.dot(rows_cot, down_mat.T, preferred_element_type=jnp.float32)
        d_gate = (d_hidden * up_act * sigmoid_gate * (1.0 + gate_act * (1.0 - sigmoid_gate))).astype(jnp.bfloat16)
        d_up = (d_hidden * gate_act * sigmoid_gate).astype(jnp.bfloat16)
        gate_grad = jnp.dot(rows_in.T, d_gate, preferred_element_type=jnp.float32)
        up_grad = jnp.dot(rows_in.T, d_up, preferred_element_type=jnp.float32)
        count = picked.shape[0]
        gate_groups = d_gate.astype(jnp.float32).reshape(count, groups, HIDDEN_DEV)
        up_groups = d_up.astype(jnp.float32).reshape(count, groups, HIDDEN_DEV)
        wg_groups = gate_mat.astype(jnp.float32).reshape(width, groups, HIDDEN_DEV)
        wu_groups = up_mat.astype(jnp.float32).reshape(width, groups, HIDDEN_DEV)
        shares = jnp.einsum('mqu,dqu->mqd', gate_groups, wg_groups) + jnp.einsum('mqu,dqu->mqd', up_groups, wu_groups)
        shares = lax.optimization_barrier(shares.astype(jnp.bfloat16)).astype(jnp.float32)
        pick_sum = jnp.sum(shares, axis=1)
        total = total.at[owner_tok].add(jnp.where(valid[:, None], pick_sum, jnp.zeros((), jnp.float32)))
        return total, (gate_grad.astype(jnp.bfloat16), up_grad.astype(jnp.bfloat16), down_grad.astype(jnp.bfloat16))

    empty = jnp.zeros(flat_rows.shape, jnp.float32)
    total, grads = lax.scan(per_expert, empty, (table, w_gate, w_up, w_down))
    grad_input = total.astype(jnp.bfloat16).reshape(tokens.shape)
    return grad_input, grads[0][matching], grads[1][matching], grads[2][matching]
```

```python
import jax
import jax.numpy as jnp
from jax import lax
from jax.experimental import pallas as pl
from jax.experimental.pallas import tpu as pltpu
from jax.sharding import PartitionSpec as P

LANES = 128
BF = jnp.bfloat16
F32 = jnp.float32


def dot(a, b, dims):
    return lax.dot_general(a, b, (dims, ((), ())), preferred_element_type=F32)


def hop(x, axis, step, size):
    return lax.ppermute(x, axis, [(i, (i + step) % size) for i in range(size)])


def flip(x, axis, bit, size):
    return lax.ppermute(x, axis, [(i, i ^ bit) for i in range(size)])


def to_chunks(x, experts, low):
    parts = x.shape[1] // LANES
    head = x[: experts * low].reshape(experts, low, parts, LANES)
    head = head.transpose(0, 2, 1, 3).reshape(experts, low * parts, LANES)
    last = x[experts * low :].reshape(experts, parts, LANES)
    pad = -(low + 1) * parts % 16
    return jnp.concatenate([head, last, jnp.zeros((experts, pad, LANES), x.dtype)], axis=1)


def from_chunks(y, experts, low, parts):
    head = y[:, : low * parts].reshape(experts, parts, low, LANES)
    head = head.transpose(0, 2, 1, 3).reshape(experts * low, parts * LANES)
    last = y[:, low * parts : (low + 1) * parts].reshape(experts, parts * LANES)
    return jnp.concatenate([head, last], axis=0)


def gather_slices(x, me, size):
    mate = flip(x, "dp", 1, size)
    own_up, own_down = hop(x, "dp", 2, size), hop(x, "dp", -2, size)
    mate_up, mate_down = hop(mate, "dp", 2, size), hop(mate, "dp", -2, size)
    own_far, mate_far = hop(own_up, "dp", 2, size), hop(mate_down, "dp", -2, size)
    return (x, mate, own_up, own_down, mate_up, mate_down, own_far, mate_far)


def slice_ids(me, size):
    mate = me ^ 1
    wrap = lambda v: v % size
    return jnp.stack(
        [me, mate, wrap(me + size - 2), wrap(me + 2), wrap(mate + size - 2), wrap(mate + 2),
         wrap(me + size - 4), wrap(mate + 4)]
    ).astype(jnp.int32)


def act_kernel(ids, *refs):
    ins, (wg, wu, gate_ref, up_ref) = refs[:8], refs[8:]
    part = ins[0].shape[1]
    for k in range(8):
        at = pl.ds(pl.multiple_of(ids[k] * part, part), part)
        rows = ins[k][...]
        g = dot(rows, wg[at, :], ((1,), (0,)))
        u = dot(rows, wu[at, :], ((1,), (0,)))
        if k == 0:
            gate_ref[...] = g
            up_ref[...] = u
        else:
            gate_ref[...] += g
            up_ref[...] += u


def share_kernel(ids, *refs):
    cots = refs[:8]
    wg, wu, wd, gate_ref, up_ref, hid_ref, dg_ref, du_ref, share_ref, acc = refs[8:]
    part = cots[0].shape[1]
    for k in range(8):
        at = pl.ds(pl.multiple_of(ids[k] * part, part), part)
        h = dot(cots[k][...], wd[:, at], ((1,), (1,)))
        if k == 0:
            acc[...] = h
        else:
            acc[...] += h
    gate, up, d_hidden = gate_ref[...], up_ref[...], acc[...]
    s = jax.nn.sigmoid(gate)
    hid_ref[...] = (gate * s * up).astype(BF)
    dg_ref[...] = (d_hidden * up * s * (1.0 + gate * (1.0 - s))).astype(BF)
    du_ref[...] = (d_hidden * gate * s).astype(BF)
    for k in range(8):
        at = pl.ds(k * part, part)
        total = dot(dg_ref[...], wg[at, :], ((1,), (1,))) + dot(du_ref[...], wu[at, :], ((1,), (1,)))
        share_ref[k] = total.astype(BF)


def grad_kernel(ids, *refs):
    ins, cots = refs[:8], refs[8:16]
    hid, dg, du, gg_ref, gu_ref, gd_ref = refs[16:]
    part = ins[0].shape[1]
    for k in range(8):
        at = pl.ds(pl.multiple_of(ids[k] * part, part), part)
        rows = ins[k][...]
        gg_ref[at, :] = dot(rows, dg[...], ((0,), (0,))).astype(BF)
        gu_ref[at, :] = dot(rows, du[...], ((0,), (0,))).astype(BF)
        gd_ref[:, at] = dot(hid[...], cots[k][...], ((0,), (0,))).astype(BF)


def call(kernel, ids, args, outs, flops, scratch=()):
    vm = pl.BlockSpec(memory_space=pltpu.VMEM)
    size = lambda a: a.size * a.dtype.itemsize
    return pl.pallas_call(
        kernel,
        out_shape=outs,
        in_specs=[pl.BlockSpec(memory_space=pltpu.SMEM)] + [vm] * len(args),
        out_specs=jax.tree.map(lambda _: vm, outs),
        scratch_shapes=list(scratch),
        compiler_params=pltpu.CompilerParams(vmem_limit_bytes=48 << 20),
        cost_estimate=pl.CostEstimate(
            flops=flops, bytes_accessed=sum(map(size, args)) + sum(map(size, outs)), transcendentals=0
        ),
    )(ids, *args)


def shards(tokens, cotangent, w_gate, w_up, w_down, routes, gates, matching):
    n_tok, width = tokens.shape[2], tokens.shape[3]
    topk = routes.shape[3]
    experts, groups = lax.axis_size("expert"), lax.axis_size("dp")
    cap = 3 * groups * n_tok * topk // (2 * experts)
    low = cap - 1
    part = width // groups
    parts = part // LANES
    hidden = w_gate.shape[2]
    me_e, me_d = lax.axis_index("expert"), lax.axis_index("dp")
    expert_iota = jnp.arange(experts, dtype=jnp.int32)
    ids = slice_ids(me_d, groups)

    flipped = jnp.sum(jnp.where(expert_iota == me_e, matching, 0)) != me_e
    swap = lambda w: jnp.where(flipped, flip(w, "expert", experts // 2, experts), w)
    wg, wu, wd = swap(w_gate[0]), swap(w_up[0]), swap(w_down[0])

    split = lambda x: x.reshape(n_tok, groups, part).transpose(1, 0, 2)
    flat_gates = gates.reshape(-1)
    meta = jnp.concatenate([routes.reshape(-1), flat_gates // 256, flat_gates % 256]).astype(F32)
    meta = jnp.pad(meta, (0, part - meta.shape[0])).astype(BF)
    meta = jnp.broadcast_to(meta[None, None], (groups, 1, part))
    stride = 32
    pad = jnp.zeros((groups, stride - 2 * n_tok - 1, part), BF)
    packed = jnp.concatenate([split(tokens[0, 0]), split(cotangent[0, 0]), meta, pad], axis=1)
    column = lax.all_to_all(packed, "dp", split_axis=0, concat_axis=0, tiled=True)
    picks = n_tok * topk
    told = column[:, 2 * n_tok, : 3 * picks].astype(F32).reshape(groups, 3, picks)
    route = told[:, 0].reshape(-1).astype(jnp.int32)
    gate_of = (told[:, 1] * 256.0 + told[:, 2]).reshape(-1) / 65536.0
    count = groups * picks

    onehot = (route[:, None] == expert_iota[None, :]).astype(BF)
    order = jnp.arange(count, dtype=jnp.int32)
    before = (order[:, None] > order[None, :]).astype(BF)
    earlier = dot(before, onehot, ((1,), (0,)))
    rank = jnp.sum(earlier * onehot.astype(F32), axis=1).astype(jnp.int32)
    target = jnp.sum(jnp.where(route[:, None] == expert_iota[None, :], matching[None, :], 0), axis=1)
    slot = jnp.where(rank < low, target * low + rank, experts * low + target)
    slot_count = experts * cap
    slots = jnp.arange(slot_count, dtype=jnp.int32)
    gate_slot = jnp.sum(jnp.where(slots[:, None] == slot[None, :], gate_of[None, :], 0.0), axis=1)
    by_tok = slot.reshape(groups, n_tok, topk)

    def places(step, first):
        spread = jnp.pad(by_tok, ((0, 0), (first, step - first - n_tok), (0, 0)), constant_values=-1)
        spread = spread.reshape(groups * step, topk)
        hit = slots[:, None] == spread[None, :, 0]
        for k in range(1, topk):
            hit = hit | (slots[:, None] == spread[None, :, k])
        return hit.astype(BF)

    rows = column.reshape(groups * stride, part)
    send_in = dot(places(stride, 0), rows, ((1,), (0,))).astype(BF)
    send_cot = (dot(places(stride, n_tok), rows, ((1,), (0,))) * gate_slot[:, None]).astype(BF)

    def exchange(x):
        x = to_chunks(x, experts, low)
        x = lax.all_to_all(x, "expert", split_axis=0, concat_axis=0, tiled=True)
        return from_chunks(x, experts, low, parts)

    ins = gather_slices(exchange(send_in), me_d, groups)
    cots = gather_slices(exchange(send_cot), me_d, groups)

    unit = 2 * slot_count * width * hidden
    act = jax.ShapeDtypeStruct((slot_count, hidden), F32)
    narrow = jax.ShapeDtypeStruct((slot_count, hidden), BF)
    gate_act, up_act = call(act_kernel, ids, (*ins, wg, wu), (act, act), 2 * unit)
    hid, dg, du, share = call(
        share_kernel,
        ids,
        (*cots, wg, wu, wd, gate_act, up_act),
        (narrow, narrow, narrow, jax.ShapeDtypeStruct((groups, slot_count, part), BF)),
        3 * unit,
        [pltpu.VMEM((slot_count, hidden), F32)],
    )
    shapes = (jax.ShapeDtypeStruct(wg.shape, BF), jax.ShapeDtypeStruct(wu.shape, BF), jax.ShapeDtypeStruct(wd.shape, BF))
    grads = call(grad_kernel, ids, (*ins, *cots, hid, dg, du), shapes, 3 * unit)

    spread = lax.all_to_all(share, "dp", split_axis=0, concat_axis=0, tiled=True)
    summed = jnp.sum(spread.astype(F32), axis=0).astype(BF)
    back = exchange(summed)
    tok_rows = 16
    total = dot(places(tok_rows, 0), back, ((0,), (0,))).astype(BF)
    home = lax.all_to_all(total.reshape(groups, tok_rows, part), "dp", split_axis=0, concat_axis=0, tiled=True)
    grad_input = home[:, :n_tok].transpose(1, 0, 2).reshape(1, 1, n_tok, width)
    return grad_input, grads[0][None], grads[1][None], grads[2][None]


def solution(mesh):
    placed = (
        P("expert", "dp", None, None),
        P("expert", "dp", None, None),
        P("expert", None, "dp"),
        P("expert", None, "dp"),
        P("expert", "dp", None),
        P("expert", "dp", None, None),
        P("expert", "dp", None, None),
        P(),
    )
    return jax.shard_map(
        shards,
        mesh=mesh,
        in_specs=placed,
        out_specs=(
            P("expert", "dp", None, None),
            P("expert", None, "dp"),
            P("expert", None, "dp"),
            P("expert", "dp", None),
        ),
        check_vma=False,
    )
```

```python
import jax
import jax.numpy as jnp
from jax import lax
from jax.experimental import pallas as pl
from jax.experimental.pallas import tpu as pltpu
from jax.sharding import PartitionSpec as P

LANES = 128
BF = jnp.bfloat16
F32 = jnp.float32


def dot(a, b, dims):
    return lax.dot_general(a, b, (dims, ((), ())), preferred_element_type=F32)


def hop(x, axis, step, size):
    return lax.ppermute(x, axis, [(i, (i + step) % size) for i in range(size)])


def flip(x, axis, bit, size):
    return lax.ppermute(x, axis, [(i, i ^ bit) for i in range(size)])


def to_chunks(x, experts, low):
    parts = x.shape[1] // LANES
    head = x[: experts * low].reshape(experts, low, parts, LANES)
    head = head.transpose(0, 2, 1, 3).reshape(experts, low * parts, LANES)
    last = x[experts * low :].reshape(experts, parts, LANES)
    pad = -(low + 1) * parts % 16
    return jnp.concatenate([head, last, jnp.zeros((experts, pad, LANES), x.dtype)], axis=1)


def from_chunks(y, experts, low, parts):
    head = y[:, : low * parts].reshape(experts, parts, low, LANES)
    head = head.transpose(0, 2, 1, 3).reshape(experts * low, parts * LANES)
    last = y[:, low * parts : (low + 1) * parts].reshape(experts, parts * LANES)
    return jnp.concatenate([head, last], axis=0)


def gather_slices(x, me, size):
    mate = flip(x, "dp", 1, size)
    own_up, own_down = hop(x, "dp", 2, size), hop(x, "dp", -2, size)
    mate_up, mate_down = hop(mate, "dp", 2, size), hop(mate, "dp", -2, size)
    own_far, mate_far = hop(own_up, "dp", 2, size), hop(mate_down, "dp", -2, size)
    return (x, mate, own_up, own_down, mate_up, mate_down, own_far, mate_far)


def slice_ids(me, size):
    mate = me ^ 1
    wrap = lambda v: v % size
    return jnp.stack(
        [me, mate, wrap(me + size - 2), wrap(me + 2), wrap(mate + size - 2), wrap(mate + 2),
         wrap(me + size - 4), wrap(mate + 4)]
    ).astype(jnp.int32)


def partial_kernel(ids, *refs):
    rows_ref, blocks, out_ref = refs[0], refs[1:-1], refs[-1]
    part = rows_ref.shape[1] // 2
    ins, cots = rows_ref[:, :part], rows_ref[:, part:]
    for k, w in enumerate(blocks):
        gate = dot(ins, w[:part, :], ((1,), (0,)))
        up = dot(ins, w[part : 2 * part, :], ((1,), (0,)))
        down = 0.0
        for q in range(part // LANES):
            tile = w[2 * part + q * LANES : 2 * part + (q + 1) * LANES, :]
            down += dot(cots[:, q * LANES : (q + 1) * LANES], tile, ((1,), (1,)))
        out_ref[ids[k]] = jnp.concatenate([gate, up, down], axis=1).astype(BF)


def point_kernel(part_ref, trio_ref, spread_ref):
    total = part_ref[0].astype(F32)
    for k in range(1, part_ref.shape[0]):
        total += part_ref[k].astype(F32)
    unit = total.shape[1] // 3
    gate, up, d_hidden = total[:, :unit], total[:, unit : 2 * unit], total[:, 2 * unit :]
    s = jax.nn.sigmoid(gate)
    hid = (gate * s * up).astype(BF)
    dg = (d_hidden * up * s * (1.0 + gate * (1.0 - s))).astype(BF)
    du = (d_hidden * gate * s).astype(BF)
    trio_ref[...] = jnp.concatenate([hid, dg, du], axis=1)
    pair = jnp.concatenate([dg, du], axis=1)
    for k in range(part_ref.shape[0]):
        spread_ref[k] = pair


def share_kernel(ids, *refs):
    pairs, blocks, out_ref, acc = refs[0], refs[1:-2], refs[-2], refs[-1]
    part = out_ref.shape[1]
    unit = pairs.shape[2] // 2
    for k, w in enumerate(blocks):
        pair = pairs[ids[k]]
        total = dot(pair[:, :unit], w[:part, :], ((1,), (1,)))
        total += dot(pair[:, unit:], w[part : 2 * part, :], ((1,), (1,)))
        if k == 0:
            acc[...] = total
        else:
            acc[...] += total
    out_ref[...] = acc[...].astype(BF)


def grad_kernel(ids, *refs):
    rows = refs[:8]
    here, there, gg_ref, gu_ref, gd_ref = refs[8:]
    part = rows[0].shape[1] // 2
    trio = jnp.where(ids[8] != 0, there[...].astype(F32), here[...].astype(F32)).astype(BF)
    unit = trio.shape[1] // 3
    hid, dg, du = trio[:, :unit], trio[:, unit : 2 * unit], trio[:, 2 * unit :]
    for k in range(8):
        at = pl.ds(pl.multiple_of(ids[k] * part, part), part)
        gg_ref[at, :] = dot(rows[k][:, :part], dg, ((0,), (0,))).astype(BF)
        gu_ref[at, :] = dot(rows[k][:, :part], du, ((0,), (0,))).astype(BF)
        gd_ref[:, at] = dot(hid, rows[k][:, part:], ((0,), (0,))).astype(BF)


def call(kernel, scalars, args, outs, flops, scratch=()):
    vm = pl.BlockSpec(memory_space=pltpu.VMEM)
    size = lambda a: a.size * a.dtype.itemsize
    return pl.pallas_call(
        kernel,
        out_shape=outs,
        in_specs=[pl.BlockSpec(memory_space=pltpu.SMEM)] * len(scalars) + [vm] * len(args),
        out_specs=jax.tree.map(lambda _: vm, outs),
        scratch_shapes=list(scratch),
        compiler_params=pltpu.CompilerParams(vmem_limit_bytes=48 << 20),
        cost_estimate=pl.CostEstimate(
            flops=flops,
            bytes_accessed=sum(map(size, args)) + sum(map(size, jax.tree.leaves(outs))),
            transcendentals=0,
        ),
    )(*scalars, *args)


def shards(tokens, cotangent, w_gate, w_up, w_down, routes, gates, matching):
    n_tok, width = tokens.shape[2], tokens.shape[3]
    topk = routes.shape[3]
    experts, groups = lax.axis_size("expert"), lax.axis_size("dp")
    cap = 3 * groups * n_tok * topk // (2 * experts)
    low = cap - 1
    part = width // groups
    parts = part // LANES
    hidden = w_gate.shape[2]
    me_e, me_d = lax.axis_index("expert"), lax.axis_index("dp")
    expert_iota = jnp.arange(experts, dtype=jnp.int32)
    flipped = jnp.sum(jnp.where(expert_iota == me_e, matching, 0)) != me_e
    ids = jnp.concatenate([slice_ids(me_d, groups), flipped.astype(jnp.int32)[None]])
    across = lambda x: flip(x, "expert", experts // 2, experts)

    def block(t):
        cut = lambda w, axis: lax.dynamic_slice_in_dim(w, t * part, part, axis)
        down = cut(w_down[0], 1).reshape(hidden, parts, LANES).transpose(1, 0, 2)
        return jnp.concatenate([cut(w_gate[0], 0), cut(w_up[0], 0), down.reshape(part, LANES)], axis=0)

    blocks = [block(me_d)] + [flip(block(me_d ^ k), "dp", k, groups) for k in range(1, groups)]
    sources = jnp.stack([me_d ^ k for k in range(groups)]).astype(jnp.int32)

    split = lambda x: x.reshape(n_tok, groups, part).transpose(1, 0, 2)
    flat_gates = gates.reshape(-1)
    meta = jnp.concatenate([routes.reshape(-1), flat_gates // 256, flat_gates % 256]).astype(F32)
    meta = jnp.pad(meta, (0, part - meta.shape[0])).astype(BF)
    meta = jnp.broadcast_to(meta[None, None], (groups, 1, part))
    stride = 32
    pad = jnp.zeros((groups, stride - 2 * n_tok - 1, part), BF)
    packed = jnp.concatenate([split(tokens[0, 0]), split(cotangent[0, 0]), meta, pad], axis=1)
    column = lax.all_to_all(packed, "dp", split_axis=0, concat_axis=0, tiled=True)
    picks = n_tok * topk
    told = column[:, 2 * n_tok, : 3 * picks].astype(F32).reshape(groups, 3, picks)
    route = told[:, 0].reshape(-1).astype(jnp.int32)
    gate_of = (told[:, 1] * 256.0 + told[:, 2]).reshape(-1) / 65536.0
    count = groups * picks

    onehot = (route[:, None] == expert_iota[None, :]).astype(BF)
    order = jnp.arange(count, dtype=jnp.int32)
    before = (order[:, None] > order[None, :]).astype(BF)
    earlier = dot(before, onehot, ((1,), (0,)))
    rank = jnp.sum(earlier * onehot.astype(F32), axis=1).astype(jnp.int32)
    slot = jnp.where(rank < low, route * low + rank, experts * low + route)
    slot_count = experts * cap
    slots = jnp.arange(slot_count, dtype=jnp.int32)
    gate_slot = jnp.sum(jnp.where(slots[:, None] == slot[None, :], gate_of[None, :], 0.0), axis=1)

    def places(step, first):
        by_tok = slot.reshape(groups, n_tok, topk)
        spread = jnp.pad(by_tok, ((0, 0), (first, step - first - n_tok), (0, 0)), constant_values=-1)
        spread = spread.reshape(groups * step, topk)
        hit = slots[:, None] == spread[None, :, 0]
        for k in range(1, topk):
            hit = hit | (slots[:, None] == spread[None, :, k])
        return hit.astype(BF)

    rows = column.reshape(groups * stride, part)
    send_in = dot(places(stride, 0), rows, ((1,), (0,))).astype(BF)
    send_cot = (dot(places(stride, n_tok), rows, ((1,), (0,))) * gate_slot[:, None]).astype(BF)

    def exchange(x):
        x = to_chunks(x, experts, low)
        return lax.all_to_all(x, "expert", split_axis=0, concat_axis=0, tiled=True)

    both = from_chunks(
        exchange(jnp.concatenate([send_in, send_cot], axis=1)), experts, low, 2 * parts
    )
    unit = 2 * slot_count * width * hidden
    sums = call(
        partial_kernel, (sources,), (both, *blocks),
        jax.ShapeDtypeStruct((groups, slot_count, 3 * hidden), BF), 3 * unit,
    )
    sums = lax.all_to_all(sums, "dp", split_axis=0, concat_axis=0, tiled=True)
    trio, pairs = call(
        point_kernel, (), (sums,),
        (
            jax.ShapeDtypeStruct((slot_count, 3 * hidden), BF),
            jax.ShapeDtypeStruct((groups, slot_count, 2 * hidden), BF),
        ), unit // 100,
    )
    pairs = lax.all_to_all(pairs, "dp", split_axis=0, concat_axis=0, tiled=True)
    share = call(
        share_kernel, (sources,), (pairs, *blocks),
        jax.ShapeDtypeStruct((slot_count, part), BF), 2 * unit,
        [pltpu.VMEM((slot_count, part), F32)],
    )

    slot_rows = gather_slices(jnp.where(flipped, across(both), both), me_d, groups)
    shapes = tuple(jax.ShapeDtypeStruct(w.shape[1:], BF) for w in (w_gate, w_up, w_down))
    grads = call(grad_kernel, (ids,), (*slot_rows, trio, across(trio)), shapes, 3 * unit)

    back = from_chunks(exchange(share), experts, low, parts)
    tok_rows = 16
    total = dot(places(tok_rows, 0), back, ((0,), (0,))).astype(BF)
    mine = lax.all_to_all(total.reshape(groups, tok_rows, part), "dp", split_axis=0, concat_axis=0, tiled=True)
    grad_input = mine[:, :n_tok].transpose(1, 0, 2).reshape(1, 1, n_tok, width)
    return grad_input, grads[0][None], grads[1][None], grads[2][None]


def solution(mesh):
    placed = (
        P("expert", "dp", None, None),
        P("expert", "dp", None, None),
        P("expert", None, "dp"),
        P("expert", None, "dp"),
        P("expert", "dp", None),
        P("expert", "dp", None, None),
        P("expert", "dp", None, None),
        P(),
    )
    return jax.shard_map(
        shards,
        mesh=mesh,
        in_specs=placed,
        out_specs=(
            P("expert", "dp", None, None),
            P("expert", None, "dp"),
            P("expert", None, "dp"),
            P("expert", "dp", None),
        ),
        check_vma=False,
    )
```

```python
import functools

import jax
import jax.numpy as jnp
from jax import lax
from jax.experimental import pallas as pl
from jax.experimental.pallas import tpu as pltpu
from jax.sharding import PartitionSpec as P

LANES = 128
BF = jnp.bfloat16
F32 = jnp.float32


def dot(a, b, dims):
    return lax.dot_general(a, b, (dims, ((), ())), preferred_element_type=F32)


def hop(x, axis, step, size):
    return lax.ppermute(x, axis, [(i, (i + step) % size) for i in range(size)])


def flip(x, axis, bit, size):
    return lax.ppermute(x, axis, [(i, i ^ bit) for i in range(size)])


def after(x, *others):
    return lax.optimization_barrier((x, *others))[0]


def pack_kernel(tok, cot, routes, gates, out):
    groups, rows, lanes = out.shape
    n_tok, topk = routes.shape
    part = (lanes - LANES) // 2
    lane = lax.broadcasted_iota(jnp.int32, (n_tok, LANES), 1)
    meta = jnp.zeros((n_tok, LANES), jnp.int32)
    for k in range(topk):
        g = gates[:, k : k + 1]
        for at, v in ((3 * k, routes[:, k : k + 1]), (3 * k + 1, g // 256), (3 * k + 2, g % 256)):
            meta = jnp.where(lane == at, v, meta)
    meta = meta.astype(F32).astype(BF)
    fill = jnp.zeros((rows - n_tok, lanes), BF)
    for d in range(groups):
        at = slice(d * part, (d + 1) * part)
        rows_here = jnp.concatenate([tok[:, at], cot[:, at], meta], axis=1)
        out[d] = jnp.concatenate([rows_here, fill], axis=0)


def block_kernel(ids, wg, wu, wd, *outs):
    part = outs[0].shape[0] // 3
    for k, out in enumerate(outs):
        start = pl.multiple_of(ids[k] * part, part)
        out[:part, :] = wg[pl.ds(start, part), :]
        out[part : 2 * part, :] = wu[pl.ds(start, part), :]
        for q in range(part // LANES):
            at = pl.ds(pl.multiple_of(start + q * LANES, LANES), LANES)
            out[2 * part + q * LANES : 2 * part + (q + 1) * LANES, :] = wd[:, at]


def route_kernel(n_tok, topk, rows_ref, out_ref, place_ref):
    groups, stride, lanes = rows_ref.shape
    experts, chunk, _ = out_ref.shape
    count = groups * stride
    cap = place_ref.shape[1] // experts
    low = cap - 1
    head = experts * low
    x = rows_ref[...].reshape(count, lanes)
    meta = x[:, lanes - LANES :].astype(F32)
    row = lax.broadcasted_iota(jnp.int32, (count, 1), 0)
    valid = row % stride < n_tok
    expert = lax.broadcasted_iota(jnp.int32, (count, experts), 1).astype(F32)
    named = [jnp.where(valid & (meta[:, 3 * k : 3 * k + 1] == expert), 1.0, 0.0) for k in range(topk)]
    every = sum(named)
    above = lax.broadcasted_iota(jnp.int32, (count, count), 0) > lax.broadcasted_iota(
        jnp.int32, (count, count), 1
    )
    earlier = dot(above.astype(F32).astype(BF), every.astype(BF), ((1,), (0,)))
    tail = chunk - low * (lanes - LANES) // LANES
    wide = lax.broadcasted_iota(jnp.int32, (count, head + experts * tail), 1)
    narrow = lax.broadcasted_iota(jnp.int32, (count, experts * cap), 1)
    pick = place = gate = None
    for k in range(topk):
        rank = jnp.sum(earlier * named[k], axis=1, keepdims=True).astype(jnp.int32)
        name = meta[:, 3 * k : 3 * k + 1].astype(jnp.int32)
        first = jnp.where(valid & (rank < low), name * low + rank, -1)
        last = jnp.where(valid & (rank >= low), name, -1)
        hit = (wide == first) | ((wide >= head) & ((wide - head) // tail == last))
        hit = jnp.where(hit, 1.0, 0.0).astype(BF)
        small = jnp.where((narrow == first) | ((narrow >= head) & (narrow - head == last)), 1.0, 0.0)
        g = dot(hit, x[:, lanes - LANES :], ((0,), (0,)))
        g = (g[:, 3 * k + 1 : 3 * k + 2] * 256.0 + g[:, 3 * k + 2 : 3 * k + 3]) * (1.0 / 65536.0)
        pick, place, gate = (hit, small, g) if k == 0 else (pick + hit, place + small, gate + g)
    place_ref[...] = place.astype(BF)
    parts = (lanes - LANES) // LANES
    slots = head + experts * tail
    spot = lax.broadcasted_iota(jnp.int32, (experts * tail, LANES), 0) % tail
    ends = jnp.zeros((experts * tail, LANES), F32)
    heads = []
    for q in range(parts):
        rows = dot(pick, x[:, q * LANES : (q + 1) * LANES], ((0,), (0,)))
        if q >= parts // 2:
            rows = rows * gate
        heads.append(rows[:head].reshape(experts, low, LANES))
        ends = jnp.where(spot == q, rows[head:], ends)
        if q % 2 == 1:
            pair = jnp.concatenate(heads, axis=1)
            out_ref[:, (q - 1) * low : (q + 1) * low, :] = pair.astype(BF)
            heads = []
    out_ref[:, parts * low :, :] = ends.reshape(experts, tail, LANES).astype(BF)


def to_chunks(x, experts, low):
    parts = x.shape[1] // LANES
    head = x[: experts * low].reshape(experts, low, parts, LANES)
    head = head.transpose(0, 2, 1, 3).reshape(experts, low * parts, LANES)
    last = x[experts * low :].reshape(experts, parts, LANES)
    pad = -(low + 1) * parts % 16
    return jnp.concatenate([head, last, jnp.zeros((experts, pad, LANES), x.dtype)], axis=1)


def from_chunks(y, experts, low, parts):
    head = y[:, : low * parts].reshape(experts, parts, low, LANES)
    head = head.transpose(0, 2, 1, 3).reshape(experts * low, parts * LANES)
    last = y[:, low * parts : (low + 1) * parts].reshape(experts, parts * LANES)
    return jnp.concatenate([head, last], axis=0)


def gather_slices(x, me, size):
    mate = flip(x, "dp", 1, size)
    own_up, own_down = hop(x, "dp", 2, size), hop(x, "dp", -2, size)
    mate_up, mate_down = hop(mate, "dp", 2, size), hop(mate, "dp", -2, size)
    own_far, mate_far = hop(own_up, "dp", 2, size), hop(mate_down, "dp", -2, size)
    return (x, mate, own_up, own_down, mate_up, mate_down, own_far, mate_far)


def slice_ids(me, size):
    mate = me ^ 1
    wrap = lambda v: v % size
    return jnp.stack(
        [me, mate, wrap(me + size - 2), wrap(me + 2), wrap(mate + size - 2), wrap(mate + 2),
         wrap(me + size - 4), wrap(mate + 4)]
    ).astype(jnp.int32)


def partial_kernel(ids, *refs):
    rows_ref, blocks, out_ref = refs[0], refs[1:-1], refs[-1]
    part = rows_ref.shape[1] // 2
    ins, cots = rows_ref[:, :part], rows_ref[:, part:]
    for k, w in enumerate(blocks):
        gate = dot(ins, w[:part, :], ((1,), (0,)))
        up = dot(ins, w[part : 2 * part, :], ((1,), (0,)))
        down = 0.0
        for q in range(part // LANES):
            tile = w[2 * part + q * LANES : 2 * part + (q + 1) * LANES, :]
            down += dot(cots[:, q * LANES : (q + 1) * LANES], tile, ((1,), (1,)))
        out_ref[ids[k]] = jnp.concatenate([gate, up, down], axis=1).astype(BF)


def point_kernel(part_ref, trio_ref, spread_ref):
    total = part_ref[0].astype(F32)
    for k in range(1, part_ref.shape[0]):
        total += part_ref[k].astype(F32)
    unit = total.shape[1] // 3
    gate, up, d_hidden = total[:, :unit], total[:, unit : 2 * unit], total[:, 2 * unit :]
    s = jax.nn.sigmoid(gate)
    hid = (gate * s * up).astype(BF)
    dg = (d_hidden * up * s * (1.0 + gate * (1.0 - s))).astype(BF)
    du = (d_hidden * gate * s).astype(BF)
    trio_ref[...] = jnp.concatenate([hid, dg, du], axis=1)
    pair = jnp.concatenate([dg, du], axis=1)
    for k in range(part_ref.shape[0]):
        spread_ref[k] = pair


def share_kernel(ids, *refs):
    pairs, blocks, out_ref, acc = refs[0], refs[1:-2], refs[-2], refs[-1]
    part = out_ref.shape[1]
    unit = pairs.shape[2] // 2
    for k, w in enumerate(blocks):
        pair = pairs[ids[k]]
        total = dot(pair[:, :unit], w[:part, :], ((1,), (1,)))
        total += dot(pair[:, unit:], w[part : 2 * part, :], ((1,), (1,)))
        if k == 0:
            acc[...] = total
        else:
            acc[...] += total
    out_ref[...] = acc[...].astype(BF)


def grad_kernel(ids, *refs):
    rows = refs[:8]
    here, there, gg_ref, gu_ref, gd_ref = refs[8:]
    part = rows[0].shape[1] // 2
    trio = jnp.where(ids[8] != 0, there[...].astype(F32), here[...].astype(F32)).astype(BF)
    unit = trio.shape[1] // 3
    hid, dg, du = trio[:, :unit], trio[:, unit : 2 * unit], trio[:, 2 * unit :]
    for k in range(8):
        at = pl.ds(pl.multiple_of(ids[k] * part, part), part)
        gg_ref[at, :] = dot(rows[k][:, :part], dg, ((0,), (0,))).astype(BF)
        gu_ref[at, :] = dot(rows[k][:, :part], du, ((0,), (0,))).astype(BF)
        gd_ref[:, at] = dot(hid, rows[k][:, part:], ((0,), (0,))).astype(BF)


def call(kernel, scalars, args, outs, flops, scratch=()):
    vm = pl.BlockSpec(memory_space=pltpu.VMEM)
    size = lambda a: a.size * a.dtype.itemsize
    return pl.pallas_call(
        kernel,
        out_shape=outs,
        in_specs=[pl.BlockSpec(memory_space=pltpu.SMEM)] * len(scalars) + [vm] * len(args),
        out_specs=jax.tree.map(lambda _: vm, outs),
        scratch_shapes=list(scratch),
        compiler_params=pltpu.CompilerParams(vmem_limit_bytes=48 << 20),
        cost_estimate=pl.CostEstimate(
            flops=flops,
            bytes_accessed=sum(map(size, args)) + sum(map(size, jax.tree.leaves(outs))),
            transcendentals=0,
        ),
    )(*scalars, *args)


def shards(tokens, cotangent, w_gate, w_up, w_down, routes, gates, matching):
    n_tok, width = tokens.shape[2], tokens.shape[3]
    topk = routes.shape[3]
    experts, groups = lax.axis_size("expert"), lax.axis_size("dp")
    cap = 3 * groups * n_tok * topk // (2 * experts)
    low = cap - 1
    part = width // groups
    parts = part // LANES
    hidden = w_gate.shape[2]
    me_e, me_d = lax.axis_index("expert"), lax.axis_index("dp")
    expert_iota = jnp.arange(experts, dtype=jnp.int32)
    flipped = jnp.sum(jnp.where(expert_iota == me_e, matching, 0)) != me_e
    ids = jnp.concatenate([slice_ids(me_d, groups), flipped.astype(jnp.int32)[None]])
    across = lambda x: flip(x, "expert", experts // 2, experts)

    slot_count = experts * cap
    stride = -(-n_tok // 16) * 16
    lanes = 2 * part + LANES

    packed = call(
        pack_kernel, (), (tokens[0, 0], cotangent[0, 0], routes[0, 0], gates[0, 0]),
        jax.ShapeDtypeStruct((groups, stride, lanes), BF), 0,
    )
    column = lax.all_to_all(packed, "dp", split_axis=0, concat_axis=0, tiled=True)

    turns = (2, 6, 1, 3, 7, 4, 5)
    sources = jnp.stack([me_d] + [me_d ^ k for k in turns]).astype(jnp.int32)
    cut = jax.ShapeDtypeStruct((3 * part, hidden), BF)
    sends = call(block_kernel, (sources,), (w_gate[0], w_up[0], w_down[0]), (cut,) * groups, 0)
    blocks = [sends[0]] + [flip(b, "dp", k, groups) for k, b in zip(turns, sends[1:])]

    chunk = 2 * parts * low + 16 * (-(-2 * parts // 16))
    to_home, places = call(
        functools.partial(route_kernel, n_tok, topk), (), (column,),
        (
            jax.ShapeDtypeStruct((experts, chunk, LANES), BF),
            jax.ShapeDtypeStruct((groups * stride, slot_count), BF),
        ), 0,
    )

    def exchange(x):
        return lax.all_to_all(x, "expert", split_axis=0, concat_axis=0, tiled=True)

    arrived = exchange(after(to_home, *blocks[1:4]))
    both = from_chunks(after(arrived, *blocks[4:6]), experts, low, 2 * parts)
    unit = 2 * slot_count * width * hidden
    sums = call(
        partial_kernel, (sources,), (both, *blocks),
        jax.ShapeDtypeStruct((groups, slot_count, 3 * hidden), BF), 3 * unit,
    )
    slot_rows = jnp.where(flipped, across(both), both)
    sums = after(sums, slot_rows)
    sums = lax.all_to_all(sums, "dp", split_axis=0, concat_axis=0, tiled=True)
    trio, pairs = call(
        point_kernel, (), (sums,),
        (
            jax.ShapeDtypeStruct((slot_count, 3 * hidden), BF),
            jax.ShapeDtypeStruct((groups, slot_count, 2 * hidden), BF),
        ), unit // 100,
    )
    pairs = lax.all_to_all(pairs, "dp", split_axis=0, concat_axis=0, tiled=True)
    ring = gather_slices(slot_rows, me_d, groups)
    pairs = after(pairs, ring[2], ring[3])
    share = call(
        share_kernel, (sources,), (pairs, *blocks),
        jax.ShapeDtypeStruct((slot_count, part), BF), 2 * unit,
        [pltpu.VMEM((slot_count, part), F32)],
    )
    shapes = tuple(jax.ShapeDtypeStruct(w.shape[1:], BF) for w in (w_gate, w_up, w_down))
    grads = call(grad_kernel, (ids,), (*ring, trio, across(trio)), shapes, 3 * unit)

    back = exchange(to_chunks(share, experts, low))
    back = from_chunks(after(back, ring[4], ring[5]), experts, low, parts)
    total = dot(places, back, ((1,), (0,))).astype(BF)
    mine = lax.all_to_all(total.reshape(groups, stride, part), "dp", split_axis=0, concat_axis=0, tiled=True)
    grad_input = mine[:, :n_tok].transpose(1, 0, 2).reshape(1, 1, n_tok, width)
    return grad_input, grads[0][None], grads[1][None], grads[2][None]


def solution(mesh):
    placed = (
        P("expert", "dp", None, None),
        P("expert", "dp", None, None),
        P("expert", None, "dp"),
        P("expert", None, "dp"),
        P("expert", "dp", None),
        P("expert", "dp", None, None),
        P("expert", "dp", None, None),
        P(),
    )
    return jax.shard_map(
        shards,
        mesh=mesh,
        in_specs=placed,
        out_specs=(
            P("expert", "dp", None, None),
            P("expert", None, "dp"),
            P("expert", None, "dp"),
            P("expert", "dp", None),
        ),
        check_vma=False,
    )
```

```python
import functools

import jax
import jax.numpy as jnp
from jax import lax
from jax.experimental import pallas as pl
from jax.experimental.pallas import tpu as pltpu
from jax.sharding import PartitionSpec as P

LANES = 128
BF = jnp.bfloat16
F32 = jnp.float32


def dot(a, b, dims):
    return lax.dot_general(a, b, (dims, ((), ())), preferred_element_type=F32)


def hop(x, axis, step, size):
    return lax.ppermute(x, axis, [(i, (i + step) % size) for i in range(size)])


def flip(x, axis, bit, size):
    return lax.ppermute(x, axis, [(i, i ^ bit) for i in range(size)])


def after(x, *others):
    return lax.optimization_barrier((x, *others))[0]


def pack_kernel(tok, cot, routes, gates, out):
    groups, rows, lanes = out.shape
    n_tok, topk = routes.shape
    part = (lanes - LANES) // 2
    lane = lax.broadcasted_iota(jnp.int32, (n_tok, LANES), 1)
    meta = jnp.zeros((n_tok, LANES), jnp.int32)
    for k in range(topk):
        g = gates[:, k : k + 1]
        for at, v in ((3 * k, routes[:, k : k + 1]), (3 * k + 1, g // 256), (3 * k + 2, g % 256)):
            meta = jnp.where(lane == at, v, meta)
    meta = meta.astype(F32).astype(BF)
    fill = jnp.zeros((rows - n_tok, lanes), BF)
    for d in range(groups):
        at = slice(d * part, (d + 1) * part)
        rows_here = jnp.concatenate([tok[:, at], cot[:, at], meta], axis=1)
        out[d] = jnp.concatenate([rows_here, fill], axis=0)


def block_kernel(ids, wg, wu, wd, *outs):
    count = len(outs) // 2
    span = outs[0].shape[0] // 2
    for k in range(count):
        start = pl.multiple_of(ids[k] * span, span)
        outs[k][:span, :] = wg[pl.ds(start, span), :]
        outs[k][span:, :] = wu[pl.ds(start, span), :]
        for q in range(span // LANES):
            at = pl.ds(pl.multiple_of(start + q * LANES, LANES), LANES)
            outs[count + k][q * LANES : (q + 1) * LANES, :] = wd[:, at]


def route_kernel(n_tok, topk, rows_ref, out_ref, place_ref):
    groups, stride, lanes = rows_ref.shape
    experts, chunk, _ = out_ref.shape
    count = groups * stride
    cap = place_ref.shape[1] // experts
    low = cap - 1
    head = experts * low
    x = rows_ref[...].reshape(count, lanes)
    meta = x[:, lanes - LANES :].astype(F32)
    row = lax.broadcasted_iota(jnp.int32, (count, 1), 0)
    valid = row % stride < n_tok
    expert = lax.broadcasted_iota(jnp.int32, (count, experts), 1).astype(F32)
    named = [jnp.where(valid & (meta[:, 3 * k : 3 * k + 1] == expert), 1.0, 0.0) for k in range(topk)]
    every = sum(named)
    above = lax.broadcasted_iota(jnp.int32, (count, count), 0) > lax.broadcasted_iota(
        jnp.int32, (count, count), 1
    )
    earlier = dot(above.astype(F32).astype(BF), every.astype(BF), ((1,), (0,)))
    tail = chunk - low * (lanes - LANES) // LANES
    wide = lax.broadcasted_iota(jnp.int32, (count, head + experts * tail), 1)
    narrow = lax.broadcasted_iota(jnp.int32, (count, experts * cap), 1)
    pick = place = gate = None
    for k in range(topk):
        rank = jnp.sum(earlier * named[k], axis=1, keepdims=True).astype(jnp.int32)
        name = meta[:, 3 * k : 3 * k + 1].astype(jnp.int32)
        first = jnp.where(valid & (rank < low), name * low + rank, -1)
        last = jnp.where(valid & (rank >= low), name, -1)
        hit = (wide == first) | ((wide >= head) & ((wide - head) // tail == last))
        hit = jnp.where(hit, 1.0, 0.0).astype(BF)
        small = jnp.where((narrow == first) | ((narrow >= head) & (narrow - head == last)), 1.0, 0.0)
        g = dot(hit, x[:, lanes - LANES :], ((0,), (0,)))
        g = (g[:, 3 * k + 1 : 3 * k + 2] * 256.0 + g[:, 3 * k + 2 : 3 * k + 3]) * (1.0 / 65536.0)
        pick, place, gate = (hit, small, g) if k == 0 else (pick + hit, place + small, gate + g)
    place_ref[...] = place.astype(BF)
    parts = (lanes - LANES) // LANES
    slots = head + experts * tail
    spot = lax.broadcasted_iota(jnp.int32, (experts * tail, LANES), 0) % tail
    ends = jnp.zeros((experts * tail, LANES), F32)
    heads = []
    for q in range(parts):
        rows = dot(pick, x[:, q * LANES : (q + 1) * LANES], ((0,), (0,)))
        if q >= parts // 2:
            rows = rows * gate
        heads.append(rows[:head].reshape(experts, low, LANES))
        ends = jnp.where(spot == q, rows[head:], ends)
        if q % 2 == 1:
            pair = jnp.concatenate(heads, axis=1)
            out_ref[:, (q - 1) * low : (q + 1) * low, :] = pair.astype(BF)
            heads = []
    out_ref[:, parts * low :, :] = ends.reshape(experts, tail, LANES).astype(BF)


def to_chunks(x, experts, low):
    parts = x.shape[1] // LANES
    head = x[: experts * low].reshape(experts, low, parts, LANES)
    head = head.transpose(0, 2, 1, 3).reshape(experts, low * parts, LANES)
    last = x[experts * low :].reshape(experts, parts, LANES)
    pad = -(low + 1) * parts % 16
    return jnp.concatenate([head, last, jnp.zeros((experts, pad, LANES), x.dtype)], axis=1)


def from_chunks(y, experts, low, parts):
    head = y[:, : low * parts].reshape(experts, parts, low, LANES)
    head = head.transpose(0, 2, 1, 3).reshape(experts * low, parts * LANES)
    last = y[:, low * parts : (low + 1) * parts].reshape(experts, parts * LANES)
    return jnp.concatenate([head, last], axis=0)


def gather_slices(x, mate, size):
    own_up, own_down = hop(x, "dp", 2, size), hop(x, "dp", -2, size)
    mate_up, mate_down = hop(mate, "dp", 2, size), hop(mate, "dp", -2, size)
    own_far, mate_far = hop(own_up, "dp", 2, size), hop(mate_down, "dp", -2, size)
    return (x, mate, own_up, own_down, mate_up, mate_down, own_far, mate_far)


def slice_ids(me, size):
    mate = me ^ 1
    wrap = lambda v: v % size
    return jnp.stack(
        [me, mate, wrap(me + size - 2), wrap(me + 2), wrap(mate + size - 2), wrap(mate + 2),
         wrap(me + size - 4), wrap(mate + 4)]
    ).astype(jnp.int32)


def partial_kernel(ids, own_ref, mate_ref, *refs):
    count = len(refs) // 3
    part = own_ref.shape[1] // 2
    for k in range(count):
        w, wd, out_ref = refs[k], refs[count + k], refs[2 * count + k]
        span = w.shape[0] // 2
        gate = up = down = 0.0
        for half, rows in ((ids[ids.shape[0] - 1], own_ref), (1 - ids[ids.shape[0] - 1], mate_ref)):
            base = half * part
            at = lambda which, n=part, off=0: pl.ds(pl.multiple_of(which * span + base + off, LANES), n)
            gate += dot(rows[:, :part], w[at(0), :], ((1,), (0,)))
            up += dot(rows[:, :part], w[at(1), :], ((1,), (0,)))
            for q in range(part // LANES):
                cots = rows[:, part + q * LANES : part + (q + 1) * LANES]
                down += dot(cots, wd[at(0, LANES, q * LANES), :], ((1,), (1,)))
        out_ref[...] = jnp.concatenate([gate, up, down], axis=1).astype(BF)


def point_kernel(*refs):
    trio_ref, pair_ref = refs[-2:]
    total = refs[0][...].astype(F32)
    for part_ref in refs[1:-2]:
        total += part_ref[...].astype(F32)
    unit = total.shape[1] // 3
    gate, up, d_hidden = total[:, :unit], total[:, unit : 2 * unit], total[:, 2 * unit :]
    s = jax.nn.sigmoid(gate)
    hid = (gate * s * up).astype(BF)
    dg = (d_hidden * up * s * (1.0 + gate * (1.0 - s))).astype(BF)
    du = (d_hidden * gate * s).astype(BF)
    trio_ref[...] = jnp.concatenate([hid, dg, du], axis=1)
    pair_ref[...] = jnp.concatenate([dg, du], axis=1)


def share_kernel(which, ids, *refs):
    out_ref, acc = refs[-2:]
    count = len(refs) // 2 - 1
    part = out_ref.shape[1]
    unit = refs[0].shape[1] // 2
    half = ids[ids.shape[0] - 1] if which == 0 else 1 - ids[ids.shape[0] - 1]
    for k in range(count):
        pair, w = refs[k], refs[count + k]
        span = w.shape[0] // 2
        at = lambda n: pl.ds(pl.multiple_of(n * span + half * part, LANES), part)
        total = dot(pair[:, :unit], w[at(0), :], ((1,), (1,)))
        total += dot(pair[:, unit:], w[at(1), :], ((1,), (1,)))
        if k == 0:
            acc[...] = total
        else:
            acc[...] += total
    out_ref[...] = acc[...].astype(out_ref.dtype)


def grad_kernel(ids, *refs):
    rows = refs[:8]
    here, there, gg_ref, gu_ref, gd_ref = refs[8:]
    part = rows[0].shape[1] // 2
    trio = jnp.where(ids[8] != 0, there[...].astype(F32), here[...].astype(F32)).astype(BF)
    unit = trio.shape[1] // 3
    hid, dg, du = trio[:, :unit], trio[:, unit : 2 * unit], trio[:, 2 * unit :]
    for k in range(8):
        at = pl.ds(pl.multiple_of(ids[k] * part, part), part)
        gg_ref[at, :] = dot(rows[k][:, :part], dg, ((0,), (0,))).astype(BF)
        gu_ref[at, :] = dot(rows[k][:, :part], du, ((0,), (0,))).astype(BF)
        gd_ref[:, at] = dot(hid, rows[k][:, part:], ((0,), (0,))).astype(BF)


def call(kernel, scalars, args, outs, flops, scratch=()):
    vm = pl.BlockSpec(memory_space=pltpu.VMEM)
    size = lambda a: a.size * a.dtype.itemsize
    return pl.pallas_call(
        kernel,
        out_shape=outs,
        in_specs=[pl.BlockSpec(memory_space=pltpu.SMEM)] * len(scalars) + [vm] * len(args),
        out_specs=jax.tree.map(lambda _: vm, outs),
        scratch_shapes=list(scratch),
        compiler_params=pltpu.CompilerParams(vmem_limit_bytes=48 << 20),
        cost_estimate=pl.CostEstimate(
            flops=flops,
            bytes_accessed=sum(map(size, args)) + sum(map(size, jax.tree.leaves(outs))),
            transcendentals=0,
        ),
    )(*scalars, *args)


def shards(tokens, cotangent, w_gate, w_up, w_down, routes, gates, matching):
    n_tok, width = tokens.shape[2], tokens.shape[3]
    topk = routes.shape[3]
    experts, groups = lax.axis_size("expert"), lax.axis_size("dp")
    cap = 3 * groups * n_tok * topk // (2 * experts)
    low = cap - 1
    part = width // groups
    parts = part // LANES
    hidden = w_gate.shape[2]
    me_e, me_d = lax.axis_index("expert"), lax.axis_index("dp")
    expert_iota = jnp.arange(experts, dtype=jnp.int32)
    flipped = jnp.sum(jnp.where(expert_iota == me_e, matching, 0)) != me_e
    ids = jnp.concatenate([slice_ids(me_d, groups), flipped.astype(jnp.int32)[None]])
    across = lambda x: flip(x, "expert", experts // 2, experts)

    slot_count = experts * cap
    stride = -(-n_tok // 16) * 16
    lanes = 2 * part + LANES

    packed = call(
        pack_kernel, (), (tokens[0, 0], cotangent[0, 0], routes[0, 0], gates[0, 0]),
        jax.ShapeDtypeStruct((groups, stride, lanes), BF), 0,
    )
    column = lax.all_to_all(packed, "dp", split_axis=0, concat_axis=0, tiled=True)

    turns = (2, 6, 4)
    ring_len = groups // 2
    sources = jnp.stack([me_d // 2] + [(me_d ^ k) // 2 for k in turns] + [me_d % 2]).astype(jnp.int32)
    cut = lambda n: (jax.ShapeDtypeStruct((n * part, hidden), BF),) * ring_len
    sends = call(block_kernel, (sources,), (w_gate[0], w_up[0], w_down[0]), cut(4) + cut(2), 0)
    arrive = lambda sent: [sent[0]] + [flip(b, "dp", k, groups) for k, b in zip(turns, sent[1:])]
    w_in, w_out = arrive(sends[:ring_len]), arrive(sends[ring_len:])

    chunk = 2 * parts * low + 16 * (-(-2 * parts // 16))
    to_home, places = call(
        functools.partial(route_kernel, n_tok, topk), (), (column,),
        (
            jax.ShapeDtypeStruct((experts, chunk, LANES), BF),
            jax.ShapeDtypeStruct((groups * stride, slot_count), BF),
        ), 0,
    )

    def exchange(x):
        return lax.all_to_all(x, "expert", split_axis=0, concat_axis=0, tiled=True)

    arrived = exchange(after(to_home, *w_in[1:3]))
    both = from_chunks(after(arrived, w_in[3]), experts, low, 2 * parts)
    mate_both = flip(both, "dp", 1, groups)
    unit = 2 * slot_count * width * hidden
    sums = call(
        partial_kernel, (sources,), (both, mate_both, *w_in, *w_out),
        (jax.ShapeDtypeStruct((slot_count, 3 * hidden), BF),) * ring_len, 3 * unit,
    )
    sums = arrive(sums)
    trio, pair = call(
        point_kernel, (), sums,
        (
            jax.ShapeDtypeStruct((slot_count, 3 * hidden), BF),
            jax.ShapeDtypeStruct((slot_count, 2 * hidden), BF),
        ), unit // 100,
    )
    flips = across(after(both, mate_both))
    pairs = arrive((after(pair, flips),) * ring_len)
    slot_rows = jnp.where(flipped, flips, both)
    slot_mate = flip(slot_rows, "dp", 1, groups)
    ring = gather_slices(after(slot_rows, *pairs), after(slot_mate, *pairs), groups)

    halves = [
        call(
            functools.partial(share_kernel, which), (sources,), (*pairs, *w_in),
            jax.ShapeDtypeStruct((slot_count, part), kind), unit,
            [pltpu.VMEM((slot_count, part), F32)],
        )
        for which, kind in ((1, BF), (0, F32))
    ]
    share = (flip(halves[0], "dp", 1, groups).astype(F32) + halves[1]).astype(BF)
    shapes = tuple(jax.ShapeDtypeStruct(w.shape[1:], BF) for w in (w_gate, w_up, w_down))
    grads = call(grad_kernel, (ids,), (*ring, trio, across(trio)), shapes, 3 * unit)

    back = exchange(to_chunks(share, experts, low))
    back = from_chunks(back, experts, low, parts)
    total = dot(places, back, ((1,), (0,))).astype(BF)
    mine = lax.all_to_all(total.reshape(groups, stride, part), "dp", split_axis=0, concat_axis=0, tiled=True)
    grad_input = mine[:, :n_tok].transpose(1, 0, 2).reshape(1, 1, n_tok, width)
    return grad_input, grads[0][None], grads[1][None], grads[2][None]


def solution(mesh):
    placed = (
        P("expert", "dp", None, None),
        P("expert", "dp", None, None),
        P("expert", None, "dp"),
        P("expert", None, "dp"),
        P("expert", "dp", None),
        P("expert", "dp", None, None),
        P("expert", "dp", None, None),
        P(),
    )
    return jax.shard_map(
        shards,
        mesh=mesh,
        in_specs=placed,
        out_specs=(
            P("expert", "dp", None, None),
            P("expert", None, "dp"),
            P("expert", None, "dp"),
            P("expert", "dp", None),
        ),
        check_vma=False,
    )
```

```python
import functools

import jax
import jax.numpy as jnp
from jax import lax
from jax.experimental import pallas as pl
from jax.experimental.pallas import tpu as pltpu
from jax.sharding import PartitionSpec as P

LANES = 128
BF = jnp.bfloat16
F32 = jnp.float32


def dot(a, b, dims):
    return lax.dot_general(a, b, (dims, ((), ())), preferred_element_type=F32)


def hop(x, axis, step, size):
    return lax.ppermute(x, axis, [(i, (i + step) % size) for i in range(size)])


def flip(x, axis, bit, size):
    return lax.ppermute(x, axis, [(i, i ^ bit) for i in range(size)])


def after(x, *others):
    return lax.optimization_barrier((x, *others))[0]


def pack_kernel(tok, cot, routes, gates, out):
    groups, rows, lanes = out.shape
    n_tok, topk = routes.shape
    part = (lanes - LANES) // 2
    lane = lax.broadcasted_iota(jnp.int32, (n_tok, LANES), 1)
    meta = jnp.zeros((n_tok, LANES), jnp.int32)
    for k in range(topk):
        g = gates[:, k : k + 1]
        for at, v in ((3 * k, routes[:, k : k + 1]), (3 * k + 1, g // 256), (3 * k + 2, g % 256)):
            meta = jnp.where(lane == at, v, meta)
    meta = meta.astype(F32).astype(BF)
    fill = jnp.zeros((rows - n_tok, lanes), BF)
    for d in range(groups):
        at = slice(d * part, (d + 1) * part)
        rows_here = jnp.concatenate([tok[:, at], cot[:, at], meta], axis=1)
        out[d] = jnp.concatenate([rows_here, fill], axis=0)


def in_kernel(ids, wg, wu, *outs):
    span = outs[0].shape[0] // 2
    for k, out in enumerate(outs):
        at = pl.ds(pl.multiple_of(ids[k] * span, span), span)
        out[:span, :] = wg[at, :]
        out[span:, :] = wu[at, :]


def out_kernel(ids, wd, *outs):
    span = outs[0].shape[0]
    for k, out in enumerate(outs):
        for q in range(span // LANES):
            at = pl.ds(pl.multiple_of(ids[k] * span + q * LANES, LANES), LANES)
            out[q * LANES : (q + 1) * LANES, :] = wd[:, at]


def route_kernel(n_tok, topk, rows_ref, out_ref, place_ref):
    groups, stride, lanes = rows_ref.shape
    experts, chunk, _ = out_ref.shape
    count = groups * stride
    cap = place_ref.shape[1] // experts
    low = cap - 1
    head = experts * low
    x = rows_ref[...].reshape(count, lanes)
    meta = x[:, lanes - LANES :].astype(F32)
    row = lax.broadcasted_iota(jnp.int32, (count, 1), 0)
    valid = row % stride < n_tok
    expert = lax.broadcasted_iota(jnp.int32, (count, experts), 1).astype(F32)
    named = [jnp.where(valid & (meta[:, 3 * k : 3 * k + 1] == expert), 1.0, 0.0) for k in range(topk)]
    every = sum(named)
    above = lax.broadcasted_iota(jnp.int32, (count, count), 0) > lax.broadcasted_iota(
        jnp.int32, (count, count), 1
    )
    earlier = dot(above.astype(F32).astype(BF), every.astype(BF), ((1,), (0,)))
    tail = chunk - low * (lanes - LANES) // LANES
    wide = lax.broadcasted_iota(jnp.int32, (count, head + experts * tail), 1)
    narrow = lax.broadcasted_iota(jnp.int32, (count, experts * cap), 1)
    pick = place = gate = None
    for k in range(topk):
        rank = jnp.sum(earlier * named[k], axis=1, keepdims=True).astype(jnp.int32)
        name = meta[:, 3 * k : 3 * k + 1].astype(jnp.int32)
        first = jnp.where(valid & (rank < low), name * low + rank, -1)
        last = jnp.where(valid & (rank >= low), name, -1)
        hit = (wide == first) | ((wide >= head) & ((wide - head) // tail == last))
        hit = jnp.where(hit, 1.0, 0.0).astype(BF)
        small = jnp.where((narrow == first) | ((narrow >= head) & (narrow - head == last)), 1.0, 0.0)
        g = dot(hit, x[:, lanes - LANES :], ((0,), (0,)))
        g = (g[:, 3 * k + 1 : 3 * k + 2] * 256.0 + g[:, 3 * k + 2 : 3 * k + 3]) * (1.0 / 65536.0)
        pick, place, gate = (hit, small, g) if k == 0 else (pick + hit, place + small, gate + g)
    place_ref[...] = place.astype(BF)
    parts = (lanes - LANES) // LANES
    slots = head + experts * tail
    spot = lax.broadcasted_iota(jnp.int32, (experts * tail, LANES), 0) % tail
    ends = jnp.zeros((experts * tail, LANES), F32)
    heads = []
    for q in range(parts):
        rows = dot(pick, x[:, q * LANES : (q + 1) * LANES], ((0,), (0,)))
        if q >= parts // 2:
            rows = rows * gate
        heads.append(rows[:head].reshape(experts, low, LANES))
        ends = jnp.where(spot == q, rows[head:], ends)
        if q % 2 == 1:
            pair = jnp.concatenate(heads, axis=1)
            out_ref[:, (q - 1) * low : (q + 1) * low, :] = pair.astype(BF)
            heads = []
    out_ref[:, parts * low :, :] = ends.reshape(experts, tail, LANES).astype(BF)


def to_chunks(x, experts, low):
    parts = x.shape[1] // LANES
    head = x[: experts * low].reshape(experts, low, parts, LANES)
    head = head.transpose(0, 2, 1, 3).reshape(experts, low * parts, LANES)
    last = x[experts * low :].reshape(experts, parts, LANES)
    pad = -(low + 1) * parts % 16
    return jnp.concatenate([head, last, jnp.zeros((experts, pad, LANES), x.dtype)], axis=1)


def from_chunks(y, experts, low, parts):
    head = y[:, : low * parts].reshape(experts, parts, low, LANES)
    head = head.transpose(0, 2, 1, 3).reshape(experts * low, parts * LANES)
    last = y[:, low * parts : (low + 1) * parts].reshape(experts, parts * LANES)
    return jnp.concatenate([head, last], axis=0)


def gather_slices(x, mate, size):
    own_up, own_down = hop(x, "dp", 2, size), hop(x, "dp", -2, size)
    mate_up, mate_down = hop(mate, "dp", 2, size), hop(mate, "dp", -2, size)
    own_far, mate_far = hop(own_up, "dp", 2, size), hop(mate_down, "dp", -2, size)
    return (x, mate, own_up, own_down, mate_up, mate_down, own_far, mate_far)


def slice_ids(me, size):
    mate = me ^ 1
    wrap = lambda v: v % size
    return jnp.stack(
        [me, mate, wrap(me + size - 2), wrap(me + 2), wrap(mate + size - 2), wrap(mate + 2),
         wrap(me + size - 4), wrap(mate + 4)]
    ).astype(jnp.int32)


def partial_kernel(ids, own_ref, mate_ref, *refs):
    count = len(refs) // 3
    part = own_ref.shape[1] // 2
    mine = ids[ids.shape[0] - 1]
    for k in range(count):
        w, wd, out_ref = refs[k::count]
        span = 2 * part
        at = lambda which, base, n: pl.ds(pl.multiple_of(which * span + base, LANES), n)
        gate = up = down = 0.0
        for half, rows in ((mine, own_ref), (1 - mine, mate_ref)):
            base = half * part
            gate += dot(rows[:, :part], w[at(0, base, part), :], ((1,), (0,)))
            up += dot(rows[:, :part], w[at(1, base, part), :], ((1,), (0,)))
            for q in range(part // LANES):
                cots = rows[:, part + q * LANES : part + (q + 1) * LANES]
                down += dot(cots, wd[at(0, base + q * LANES, LANES), :], ((1,), (1,)))
        out_ref[...] = jnp.concatenate([gate, up, down], axis=1).astype(BF)


def point_kernel(*refs):
    trio_ref, pair_ref = refs[-2:]
    total = refs[0][...].astype(F32)
    for part_ref in refs[1:-2]:
        total += part_ref[...].astype(F32)
    unit = total.shape[1] // 3
    gate, up, d_hidden = total[:, :unit], total[:, unit : 2 * unit], total[:, 2 * unit :]
    s = jax.nn.sigmoid(gate)
    hid = (gate * s * up).astype(BF)
    dg = (d_hidden * up * s * (1.0 + gate * (1.0 - s))).astype(BF)
    du = (d_hidden * gate * s).astype(BF)
    trio_ref[...] = jnp.concatenate([hid, dg, du], axis=1)
    pair_ref[...] = jnp.concatenate([dg, du], axis=1)


def share_kernel(which, ids, *refs):
    out_ref, acc = refs[-2:]
    count = len(refs) // 2 - 1
    part = out_ref.shape[1]
    unit = refs[0].shape[1] // 2
    mine = ids[ids.shape[0] - 1]
    base = (mine if which == 0 else 1 - mine) * part
    for k in range(count):
        pair, w = refs[:-2][k::count]
        at = lambda which: pl.ds(pl.multiple_of(which * 2 * part + base, LANES), part)
        total = dot(pair[:, :unit], w[at(0), :], ((1,), (1,)))
        total += dot(pair[:, unit:], w[at(1), :], ((1,), (1,)))
        if k == 0:
            acc[...] = total
        else:
            acc[...] += total
    out_ref[...] = acc[...].astype(out_ref.dtype)


def grad_kernel(ids, *refs):
    rows = refs[:8]
    here, there, gg_ref, gu_ref, gd_ref = refs[8:]
    part = rows[0].shape[1] // 2
    trio = jnp.where(ids[8] != 0, there[...].astype(F32), here[...].astype(F32)).astype(BF)
    unit = trio.shape[1] // 3
    hid, dg, du = trio[:, :unit], trio[:, unit : 2 * unit], trio[:, 2 * unit :]
    for k in range(8):
        at = pl.ds(pl.multiple_of(ids[k] * part, part), part)
        gg_ref[at, :] = dot(rows[k][:, :part], dg, ((0,), (0,))).astype(BF)
        gu_ref[at, :] = dot(rows[k][:, :part], du, ((0,), (0,))).astype(BF)
        gd_ref[:, at] = dot(hid, rows[k][:, part:], ((0,), (0,))).astype(BF)


def call(kernel, scalars, args, outs, flops, scratch=()):
    vm = pl.BlockSpec(memory_space=pltpu.VMEM)
    size = lambda a: a.size * a.dtype.itemsize
    return pl.pallas_call(
        kernel,
        out_shape=outs,
        in_specs=[pl.BlockSpec(memory_space=pltpu.SMEM)] * len(scalars) + [vm] * len(args),
        out_specs=jax.tree.map(lambda _: vm, outs),
        scratch_shapes=list(scratch),
        compiler_params=pltpu.CompilerParams(vmem_limit_bytes=48 << 20),
        cost_estimate=pl.CostEstimate(
            flops=flops,
            bytes_accessed=sum(map(size, args)) + sum(map(size, jax.tree.leaves(outs))),
            transcendentals=0,
        ),
    )(*scalars, *args)


def shards(tokens, cotangent, w_gate, w_up, w_down, routes, gates, matching):
    n_tok, width = tokens.shape[2], tokens.shape[3]
    topk = routes.shape[3]
    experts, groups = lax.axis_size("expert"), lax.axis_size("dp")
    cap = 3 * groups * n_tok * topk // (2 * experts)
    low = cap - 1
    part = width // groups
    parts = part // LANES
    hidden = w_gate.shape[2]
    me_e, me_d = lax.axis_index("expert"), lax.axis_index("dp")
    expert_iota = jnp.arange(experts, dtype=jnp.int32)
    flipped = jnp.sum(jnp.where(expert_iota == me_e, matching, 0)) != me_e
    ids = jnp.concatenate([slice_ids(me_d, groups), flipped.astype(jnp.int32)[None]])
    across = lambda x: flip(x, "expert", experts // 2, experts)

    slot_count = experts * cap
    stride = -(-n_tok // 16) * 16
    lanes = 2 * part + LANES

    packed = call(
        pack_kernel, (), (tokens[0, 0], cotangent[0, 0], routes[0, 0], gates[0, 0]),
        jax.ShapeDtypeStruct((groups, stride, lanes), BF), 0,
    )
    column = lax.all_to_all(packed, "dp", split_axis=0, concat_axis=0, tiled=True)

    turns = (2, 6, 4)
    ring_len = groups // 2
    sources = jnp.stack([me_d // 2] + [(me_d ^ k) // 2 for k in turns] + [me_d % 2]).astype(jnp.int32)
    chunk = 2 * parts * low + 16 * (-(-2 * parts // 16))
    def route(rows):
        return call(
            functools.partial(route_kernel, n_tok, topk), (), (rows,),
            (
                jax.ShapeDtypeStruct((experts, chunk, LANES), BF),
                jax.ShapeDtypeStruct((groups * stride, slot_count), BF),
            ), 0,
        )

    arrive = lambda sent: [sent[0]] + [flip(b, "dp", k, groups) for k, b in zip(turns, sent[1:])]
    cut = lambda n: (jax.ShapeDtypeStruct((n * part, hidden), BF),) * ring_len
    w_out = arrive(call(out_kernel, (after(sources, packed),), (w_down[0],), cut(2), 0))
    to_home, places = route(column)
    w_in = arrive(call(in_kernel, (after(sources, to_home),), (w_gate[0], w_up[0]), cut(4), 0))

    def exchange(x):
        return lax.all_to_all(x, "expert", split_axis=0, concat_axis=0, tiled=True)

    arrived = exchange(after(to_home, *w_out[1:3]))
    both = from_chunks(after(arrived, w_out[3], *w_in[1:3]), experts, low, 2 * parts)
    mate_both = flip(both, "dp", 1, groups)
    unit = 2 * slot_count * width * hidden
    sums = call(
        partial_kernel, (sources,), (both, mate_both, *w_in, *w_out),
        (jax.ShapeDtypeStruct((slot_count, 3 * hidden), BF),) * ring_len, 3 * unit,
    )
    sums = arrive(sums)
    trio, pair = call(
        point_kernel, (), sums,
        (
            jax.ShapeDtypeStruct((slot_count, 3 * hidden), BF),
            jax.ShapeDtypeStruct((slot_count, 2 * hidden), BF),
        ), unit // 100,
    )
    here, there = (both, mate_both), [across(after(v, mate_both)) for v in (both, mate_both)]
    pairs = arrive((pair,) * ring_len)
    pairs = lax.optimization_barrier((*pairs, there[0]))[:ring_len]
    slots = [jnp.where(flipped, a, b) for a, b in zip(there, here)]
    ring = gather_slices(after(slots[0], *pairs), slots[1], groups)

    halves = [
        call(
            functools.partial(share_kernel, which), (sources,), (*pairs, *w_in),
            jax.ShapeDtypeStruct((slot_count, part), kind), unit,
            [pltpu.VMEM((slot_count, part), F32)],
        )
        for which, kind in ((1, BF), (0, F32))
    ]
    share = (flip(halves[0], "dp", 1, groups).astype(F32) + halves[1]).astype(BF)
    share = after(share, there[1])
    shapes = tuple(jax.ShapeDtypeStruct(w.shape[1:], BF) for w in (w_gate, w_up, w_down))
    grads = call(grad_kernel, (ids,), (*ring, trio, across(trio)), shapes, 3 * unit)

    back = exchange(to_chunks(share, experts, low))
    back = from_chunks(back, experts, low, parts)
    total = dot(places, back, ((1,), (0,))).astype(BF)
    mine = lax.all_to_all(total.reshape(groups, stride, part), "dp", split_axis=0, concat_axis=0, tiled=True)
    grad_input = mine[:, :n_tok].transpose(1, 0, 2).reshape(1, 1, n_tok, width)
    return grad_input, grads[0][None], grads[1][None], grads[2][None]


def solution(mesh):
    placed = (
        P("expert", "dp", None, None),
        P("expert", "dp", None, None),
        P("expert", None, "dp"),
        P("expert", None, "dp"),
        P("expert", "dp", None),
        P("expert", "dp", None, None),
        P("expert", "dp", None, None),
        P(),
    )
    return jax.shard_map(
        shards,
        mesh=mesh,
        in_specs=placed,
        out_specs=(
            P("expert", "dp", None, None),
            P("expert", None, "dp"),
            P("expert", None, "dp"),
            P("expert", "dp", None),
        ),
        check_vma=False,
    )
```

```python
import functools

import jax
import jax.numpy as jnp
from jax import lax
from jax.experimental import pallas as pl
from jax.experimental.pallas import tpu as pltpu
from jax.sharding import PartitionSpec as P

LANES = 128
BF = jnp.bfloat16
F32 = jnp.float32


def dot(a, b, dims):
    return lax.dot_general(a, b, (dims, ((), ())), preferred_element_type=F32)


def hop(x, axis, step, size):
    return lax.ppermute(x, axis, [(i, (i + step) % size) for i in range(size)])


def flip(x, axis, bit, size):
    return lax.ppermute(x, axis, [(i, i ^ bit) for i in range(size)])


def after(x, *others):
    return lax.optimization_barrier((x, *others))[0]


def pack_kernel(tok, cot, routes, gates, out):
    groups, rows, lanes = out.shape
    n_tok, topk = routes.shape
    part = (lanes - LANES) // 2
    lane = lax.broadcasted_iota(jnp.int32, (n_tok, LANES), 1)
    meta = jnp.zeros((n_tok, LANES), jnp.int32)
    for k in range(topk):
        g = gates[:, k : k + 1]
        for at, v in ((3 * k, routes[:, k : k + 1]), (3 * k + 1, g // 256), (3 * k + 2, g % 256)):
            meta = jnp.where(lane == at, v, meta)
    meta = meta.astype(F32).astype(BF)
    fill = jnp.zeros((rows - n_tok, lanes), BF)
    for d in range(groups):
        at = slice(d * part, (d + 1) * part)
        rows_here = jnp.concatenate([tok[:, at], cot[:, at], meta], axis=1)
        out[d] = jnp.concatenate([rows_here, fill], axis=0)


def block_kernel(ids, wg, wu, wd, *outs):
    span = outs[0].shape[0] // 3
    for k, out in enumerate(outs):
        start = pl.multiple_of(ids[k] * span, span)
        out[:span, :] = wg[pl.ds(start, span), :]
        out[span : 2 * span, :] = wu[pl.ds(start, span), :]
        for q in range(span // LANES):
            at = pl.ds(pl.multiple_of(start + q * LANES, LANES), LANES)
            out[2 * span + q * LANES : 2 * span + (q + 1) * LANES, :] = wd[:, at]


def route_kernel(n_tok, topk, rows_ref, out_ref, place_ref):
    groups, stride, lanes = rows_ref.shape
    experts, chunk, _ = out_ref.shape
    count = groups * stride
    cap = place_ref.shape[1] // experts
    low = cap - 1
    head = experts * low
    x = rows_ref[...].reshape(count, lanes)
    meta = x[:, lanes - LANES :].astype(F32)
    row = lax.broadcasted_iota(jnp.int32, (count, 1), 0)
    valid = row % stride < n_tok
    expert = lax.broadcasted_iota(jnp.int32, (count, experts), 1).astype(F32)
    named = [jnp.where(valid & (meta[:, 3 * k : 3 * k + 1] == expert), 1.0, 0.0) for k in range(topk)]
    every = sum(named)
    above = lax.broadcasted_iota(jnp.int32, (count, count), 0) > lax.broadcasted_iota(
        jnp.int32, (count, count), 1
    )
    earlier = dot(above.astype(F32).astype(BF), every.astype(BF), ((1,), (0,)))
    tail = chunk - low * (lanes - LANES) // LANES
    wide = lax.broadcasted_iota(jnp.int32, (count, head + experts * tail), 1)
    narrow = lax.broadcasted_iota(jnp.int32, (count, experts * cap), 1)
    pick = place = gate = None
    for k in range(topk):
        rank = jnp.sum(earlier * named[k], axis=1, keepdims=True).astype(jnp.int32)
        name = meta[:, 3 * k : 3 * k + 1].astype(jnp.int32)
        first = jnp.where(valid & (rank < low), name * low + rank, -1)
        last = jnp.where(valid & (rank >= low), name, -1)
        hit = (wide == first) | ((wide >= head) & ((wide - head) // tail == last))
        hit = jnp.where(hit, 1.0, 0.0).astype(BF)
        small = jnp.where((narrow == first) | ((narrow >= head) & (narrow - head == last)), 1.0, 0.0)
        g = dot(hit, x[:, lanes - LANES :], ((0,), (0,)))
        g = (g[:, 3 * k + 1 : 3 * k + 2] * 256.0 + g[:, 3 * k + 2 : 3 * k + 3]) * (1.0 / 65536.0)
        pick, place, gate = (hit, small, g) if k == 0 else (pick + hit, place + small, gate + g)
    place_ref[...] = place.astype(BF)
    parts = (lanes - LANES) // LANES
    slots = head + experts * tail
    spot = lax.broadcasted_iota(jnp.int32, (experts * tail, LANES), 0) % tail
    ends = jnp.zeros((experts * tail, LANES), F32)
    heads = []
    for q in range(parts):
        rows = dot(pick, x[:, q * LANES : (q + 1) * LANES], ((0,), (0,)))
        if q >= parts // 2:
            rows = rows * gate
        heads.append(rows[:head].reshape(experts, low, LANES))
        ends = jnp.where(spot == q, rows[head:], ends)
        if q % 2 == 1:
            pair = jnp.concatenate(heads, axis=1)
            out_ref[:, (q - 1) * low : (q + 1) * low, :] = pair.astype(BF)
            heads = []
    out_ref[:, parts * low :, :] = ends.reshape(experts, tail, LANES).astype(BF)


def to_chunks(x, experts, low):
    parts = x.shape[1] // LANES
    head = x[: experts * low].reshape(experts, low, parts, LANES)
    head = head.transpose(0, 2, 1, 3).reshape(experts, low * parts, LANES)
    last = x[experts * low :].reshape(experts, parts, LANES)
    pad = -(low + 1) * parts % 16
    return jnp.concatenate([head, last, jnp.zeros((experts, pad, LANES), x.dtype)], axis=1)


def from_chunks(y, experts, low, parts):
    head = y[:, : low * parts].reshape(experts, parts, low, LANES)
    head = head.transpose(0, 2, 1, 3).reshape(experts * low, parts * LANES)
    last = y[:, low * parts : (low + 1) * parts].reshape(experts, parts * LANES)
    return jnp.concatenate([head, last], axis=0)


def gather_slices(x, mate, size):
    own_up, own_down = hop(x, "dp", 2, size), hop(x, "dp", -2, size)
    mate_up, mate_down = hop(mate, "dp", 2, size), hop(mate, "dp", -2, size)
    own_far, mate_far = hop(own_up, "dp", 2, size), hop(mate_down, "dp", -2, size)
    return (x, mate, own_up, own_down, mate_up, mate_down, own_far, mate_far)


def slice_ids(me, size):
    mate = me ^ 1
    wrap = lambda v: v % size
    return jnp.stack(
        [me, mate, wrap(me + size - 2), wrap(me + 2), wrap(mate + size - 2), wrap(mate + 2),
         wrap(me + size - 4), wrap(mate + 4)]
    ).astype(jnp.int32)


def partial_kernel(ids, own_ref, mate_ref, *refs):
    count = len(refs) // 2
    part = own_ref.shape[1] // 2
    mine = ids[ids.shape[0] - 1]
    for k in range(count):
        w, out_ref = refs[k::count]
        span = w.shape[0] // 3
        at = lambda which, base, n: pl.ds(pl.multiple_of(which * span + base, LANES), n)
        gate = up = down = 0.0
        for half, rows in ((mine, own_ref), (1 - mine, mate_ref)):
            base = half * part
            gate += dot(rows[:, :part], w[at(0, base, part), :], ((1,), (0,)))
            up += dot(rows[:, :part], w[at(1, base, part), :], ((1,), (0,)))
            for q in range(part // LANES):
                cots = rows[:, part + q * LANES : part + (q + 1) * LANES]
                down += dot(cots, w[at(2, base + q * LANES, LANES), :], ((1,), (1,)))
        out_ref[...] = jnp.concatenate([gate, up, down], axis=1).astype(BF)


def point_kernel(*refs):
    trio_ref, pair_ref = refs[-2:]
    total = refs[0][...].astype(F32)
    for part_ref in refs[1:-2]:
        total += part_ref[...].astype(F32)
    unit = total.shape[1] // 3
    gate, up, d_hidden = total[:, :unit], total[:, unit : 2 * unit], total[:, 2 * unit :]
    s = jax.nn.sigmoid(gate)
    hid = (gate * s * up).astype(BF)
    dg = (d_hidden * up * s * (1.0 + gate * (1.0 - s))).astype(BF)
    du = (d_hidden * gate * s).astype(BF)
    trio_ref[...] = jnp.concatenate([hid, dg, du], axis=1)
    pair_ref[...] = jnp.concatenate([dg, du], axis=1)


def share_kernel(which, ids, *refs):
    out_ref, acc = refs[-2:]
    count = len(refs) // 2 - 1
    part = out_ref.shape[1]
    unit = refs[0].shape[1] // 2
    mine = ids[ids.shape[0] - 1]
    base = (mine if which == 0 else 1 - mine) * part
    for k in range(count):
        pair, w = refs[:-2][k::count]
        at = lambda which: pl.ds(pl.multiple_of(which * (w.shape[0] // 3) + base, LANES), part)
        total = dot(pair[:, :unit], w[at(0), :], ((1,), (1,)))
        total += dot(pair[:, unit:], w[at(1), :], ((1,), (1,)))
        if k == 0:
            acc[...] = total
        else:
            acc[...] += total
    out_ref[...] = acc[...].astype(out_ref.dtype)


def grad_kernel(ids, *refs):
    rows = refs[:8]
    here, there, gg_ref, gu_ref, gd_ref = refs[8:]
    part = rows[0].shape[1] // 2
    trio = jnp.where(ids[8] != 0, there[...].astype(F32), here[...].astype(F32)).astype(BF)
    unit = trio.shape[1] // 3
    hid, dg, du = trio[:, :unit], trio[:, unit : 2 * unit], trio[:, 2 * unit :]
    for k in range(8):
        at = pl.ds(pl.multiple_of(ids[k] * part, part), part)
        gg_ref[at, :] = dot(rows[k][:, :part], dg, ((0,), (0,))).astype(BF)
        gu_ref[at, :] = dot(rows[k][:, :part], du, ((0,), (0,))).astype(BF)
        gd_ref[:, at] = dot(hid, rows[k][:, part:], ((0,), (0,))).astype(BF)


def call(kernel, scalars, args, outs, flops, scratch=()):
    vm = pl.BlockSpec(memory_space=pltpu.VMEM)
    size = lambda a: a.size * a.dtype.itemsize
    return pl.pallas_call(
        kernel,
        out_shape=outs,
        in_specs=[pl.BlockSpec(memory_space=pltpu.SMEM)] * len(scalars) + [vm] * len(args),
        out_specs=jax.tree.map(lambda _: vm, outs),
        scratch_shapes=list(scratch),
        compiler_params=pltpu.CompilerParams(vmem_limit_bytes=48 << 20),
        cost_estimate=pl.CostEstimate(
            flops=flops,
            bytes_accessed=sum(map(size, args)) + sum(map(size, jax.tree.leaves(outs))),
            transcendentals=0,
        ),
    )(*scalars, *args)


def shards(tokens, cotangent, w_gate, w_up, w_down, routes, gates, matching):
    n_tok, width = tokens.shape[2], tokens.shape[3]
    topk = routes.shape[3]
    experts, groups = lax.axis_size("expert"), lax.axis_size("dp")
    cap = 3 * groups * n_tok * topk // (2 * experts)
    low = cap - 1
    part = width // groups
    parts = part // LANES
    hidden = w_gate.shape[2]
    me_e, me_d = lax.axis_index("expert"), lax.axis_index("dp")
    expert_iota = jnp.arange(experts, dtype=jnp.int32)
    flipped = jnp.sum(jnp.where(expert_iota == me_e, matching, 0)) != me_e
    ids = jnp.concatenate([slice_ids(me_d, groups), flipped.astype(jnp.int32)[None]])
    across = lambda x: flip(x, "expert", experts // 2, experts)

    slot_count = experts * cap
    stride = -(-n_tok // 16) * 16
    lanes = 2 * part + LANES

    packed = call(
        pack_kernel, (), (tokens[0, 0], cotangent[0, 0], routes[0, 0], gates[0, 0]),
        jax.ShapeDtypeStruct((groups, stride, lanes), BF), 0,
    )
    column = lax.all_to_all(packed, "dp", split_axis=0, concat_axis=0, tiled=True)

    turns = (2, 6, 4)
    ring_len = groups // 2
    sources = jnp.stack([me_d // 2] + [(me_d ^ k) // 2 for k in turns] + [me_d % 2]).astype(jnp.int32)
    chunk = 2 * parts * low + 16 * (-(-2 * parts // 16))
    def route(rows):
        return call(
            functools.partial(route_kernel, n_tok, topk), (), (rows,),
            (
                jax.ShapeDtypeStruct((experts, chunk, LANES), BF),
                jax.ShapeDtypeStruct((groups * stride, slot_count), BF),
            ), 0,
        )

    to_home, places = route(column)

    cut = (jax.ShapeDtypeStruct((6 * part, hidden), BF),) * ring_len
    sends = call(block_kernel, (after(sources, to_home),), (w_gate[0], w_up[0], w_down[0]), cut, 0)
    arrive = lambda sent: [sent[0]] + [flip(b, "dp", k, groups) for k, b in zip(turns, sent[1:])]
    blocks = arrive(sends)

    def exchange(x):
        return lax.all_to_all(x, "expert", split_axis=0, concat_axis=0, tiled=True)

    arrived = exchange(to_home)
    both = from_chunks(after(arrived, *blocks[1:3]), experts, low, 2 * parts)
    mate_both = flip(both, "dp", 1, groups)
    unit = 2 * slot_count * width * hidden
    sums = call(
        partial_kernel, (sources,), (both, mate_both, *blocks),
        (jax.ShapeDtypeStruct((slot_count, 3 * hidden), BF),) * ring_len, 3 * unit,
    )
    sums = arrive(sums)
    trio, pair = call(
        point_kernel, (), sums,
        (
            jax.ShapeDtypeStruct((slot_count, 3 * hidden), BF),
            jax.ShapeDtypeStruct((slot_count, 2 * hidden), BF),
        ), unit // 100,
    )
    here, there = (both, mate_both), [across(after(v, mate_both)) for v in (both, mate_both)]
    pairs = arrive((pair,) * ring_len)
    pairs = lax.optimization_barrier((*pairs, there[0]))[:ring_len]
    slots = [jnp.where(flipped, a, b) for a, b in zip(there, here)]
    ring = gather_slices(after(slots[0], *pairs), slots[1], groups)

    halves = [
        call(
            functools.partial(share_kernel, which), (sources,), (*pairs, *blocks),
            jax.ShapeDtypeStruct((slot_count, part), kind), unit,
            [pltpu.VMEM((slot_count, part), F32)],
        )
        for which, kind in ((1, BF), (0, F32))
    ]
    share = (flip(halves[0], "dp", 1, groups).astype(F32) + halves[1]).astype(BF)
    share = after(share, there[1], ring[2], ring[3])
    shapes = tuple(jax.ShapeDtypeStruct(w.shape[1:], BF) for w in (w_gate, w_up, w_down))
    grads = call(grad_kernel, (ids,), (*ring, trio, across(trio)), shapes, 3 * unit)

    back = exchange(to_chunks(share, experts, low))
    back = from_chunks(after(back, ring[4], ring[5]), experts, low, parts)
    total = dot(places, back, ((1,), (0,))).astype(BF)
    mine = lax.all_to_all(total.reshape(groups, stride, part), "dp", split_axis=0, concat_axis=0, tiled=True)
    grad_input = mine[:, :n_tok].transpose(1, 0, 2).reshape(1, 1, n_tok, width)
    return grad_input, grads[0][None], grads[1][None], grads[2][None]


def solution(mesh):
    placed = (
        P("expert", "dp", None, None),
        P("expert", "dp", None, None),
        P("expert", None, "dp"),
        P("expert", None, "dp"),
        P("expert", "dp", None),
        P("expert", "dp", None, None),
        P("expert", "dp", None, None),
        P(),
    )
    return jax.shard_map(
        shards,
        mesh=mesh,
        in_specs=placed,
        out_specs=(
            P("expert", "dp", None, None),
            P("expert", None, "dp"),
            P("expert", None, "dp"),
            P("expert", "dp", None),
        ),
        check_vma=False,
    )
```

```python
import functools

import jax
import jax.numpy as jnp
from jax import lax
from jax.experimental import pallas as pl
from jax.experimental.pallas import tpu as pltpu
from jax.sharding import PartitionSpec as P

LANES = 128
BF = jnp.bfloat16
F32 = jnp.float32
SPAN_HINT = 14 * 10**9


def dot(a, b, dims):
    return lax.dot_general(a, b, (dims, ((), ())), preferred_element_type=F32)


def hop(x, axis, step, size):
    return lax.ppermute(x, axis, [(i, (i + step) % size) for i in range(size)])


def flip(x, axis, bit, size):
    return lax.ppermute(x, axis, [(i, i ^ bit) for i in range(size)])


def after(x, *others):
    return lax.optimization_barrier((x, *others))[0]


def pack_kernel(tok, cot, routes, gates, out):
    groups, rows, lanes = out.shape
    n_tok, topk = routes.shape
    part = (lanes - LANES) // 2
    lane = lax.broadcasted_iota(jnp.int32, (n_tok, LANES), 1)
    meta = jnp.zeros((n_tok, LANES), jnp.int32)
    for k in range(topk):
        g = gates[:, k : k + 1]
        for at, v in ((3 * k, routes[:, k : k + 1]), (3 * k + 1, g // 256), (3 * k + 2, g % 256)):
            meta = jnp.where(lane == at, v, meta)
    meta = meta.astype(F32).astype(BF)
    fill = jnp.zeros((rows - n_tok, lanes), BF)
    for d in range(groups):
        at = slice(d * part, (d + 1) * part)
        rows_here = jnp.concatenate([tok[:, at], cot[:, at], meta], axis=1)
        out[d] = jnp.concatenate([rows_here, fill], axis=0)


def block_kernel(ids, wg, wu, wd, *outs):
    span = outs[0].shape[0]
    unit = wg.shape[1]
    for k, out in enumerate(outs):
        start = pl.multiple_of(ids[k] * span, span)
        out[:, :unit] = wg[pl.ds(start, span), :]
        out[:, unit : 2 * unit] = wu[pl.ds(start, span), :]
        for q in range(span // LANES):
            at = pl.ds(pl.multiple_of(start + q * LANES, LANES), LANES)
            out[q * LANES : (q + 1) * LANES, 2 * unit :] = wd[:, at]


def route_kernel(n_tok, topk, rows_ref, out_ref, place_ref):
    groups, stride, lanes = rows_ref.shape
    experts, chunk, _ = out_ref.shape
    count = groups * stride
    cap = place_ref.shape[1] // experts
    low = cap - 1
    head = experts * low
    x = rows_ref[...].reshape(count, lanes)
    meta = x[:, lanes - LANES :].astype(F32)
    row = lax.broadcasted_iota(jnp.int32, (count, 1), 0)
    valid = row % stride < n_tok
    expert = lax.broadcasted_iota(jnp.int32, (count, experts), 1).astype(F32)
    named = [jnp.where(valid & (meta[:, 3 * k : 3 * k + 1] == expert), 1.0, 0.0) for k in range(topk)]
    every = sum(named)
    above = lax.broadcasted_iota(jnp.int32, (count, count), 0) > lax.broadcasted_iota(
        jnp.int32, (count, count), 1
    )
    earlier = dot(above.astype(F32).astype(BF), every.astype(BF), ((1,), (0,)))
    tail = chunk - low * (lanes - LANES) // LANES
    wide = lax.broadcasted_iota(jnp.int32, (count, head + experts * tail), 1)
    narrow = lax.broadcasted_iota(jnp.int32, (count, experts * cap), 1)
    pick = place = gate = None
    for k in range(topk):
        rank = jnp.sum(earlier * named[k], axis=1, keepdims=True).astype(jnp.int32)
        name = meta[:, 3 * k : 3 * k + 1].astype(jnp.int32)
        first = jnp.where(valid & (rank < low), name * low + rank, -1)
        last = jnp.where(valid & (rank >= low), name, -1)
        hit = (wide == first) | ((wide >= head) & ((wide - head) // tail == last))
        hit = jnp.where(hit, 1.0, 0.0).astype(BF)
        small = jnp.where((narrow == first) | ((narrow >= head) & (narrow - head == last)), 1.0, 0.0)
        g = dot(hit, x[:, lanes - LANES :], ((0,), (0,)))
        g = (g[:, 3 * k + 1 : 3 * k + 2] * 256.0 + g[:, 3 * k + 2 : 3 * k + 3]) * (1.0 / 65536.0)
        pick, place, gate = (hit, small, g) if k == 0 else (pick + hit, place + small, gate + g)
    place_ref[...] = place.astype(BF)
    parts = (lanes - LANES) // LANES
    slots = head + experts * tail
    spot = lax.broadcasted_iota(jnp.int32, (experts * tail, LANES), 0) % tail
    ends = jnp.zeros((experts * tail, LANES), F32)
    heads = []
    for q in range(parts):
        rows = dot(pick, x[:, q * LANES : (q + 1) * LANES], ((0,), (0,)))
        if q >= parts // 2:
            rows = rows * gate
        heads.append(rows[:head].reshape(experts, low, LANES))
        ends = jnp.where(spot == q, rows[head:], ends)
        if q % 2 == 1:
            pair = jnp.concatenate(heads, axis=1)
            out_ref[:, (q - 1) * low : (q + 1) * low, :] = pair.astype(BF)
            heads = []
    out_ref[:, parts * low :, :] = ends.reshape(experts, tail, LANES).astype(BF)


def to_chunks(x, experts, low):
    parts = x.shape[1] // LANES
    head = x[: experts * low].reshape(experts, low, parts, LANES)
    head = head.transpose(0, 2, 1, 3).reshape(experts, low * parts, LANES)
    last = x[experts * low :].reshape(experts, parts, LANES)
    pad = -(low + 1) * parts % 16
    return jnp.concatenate([head, last, jnp.zeros((experts, pad, LANES), x.dtype)], axis=1)


def from_chunks(y, experts, low, parts):
    head = y[:, : low * parts].reshape(experts, parts, low, LANES)
    head = head.transpose(0, 2, 1, 3).reshape(experts * low, parts * LANES)
    last = y[:, low * parts : (low + 1) * parts].reshape(experts, parts * LANES)
    return jnp.concatenate([head, last], axis=0)


def gather_slices(x, mate, size):
    own_up, own_down = hop(x, "dp", 2, size), hop(x, "dp", -2, size)
    mate_up, mate_down = hop(mate, "dp", 2, size), hop(mate, "dp", -2, size)
    own_far, mate_far = hop(own_up, "dp", 2, size), hop(mate_down, "dp", -2, size)
    return (x, mate, own_up, own_down, mate_up, mate_down, own_far, mate_far)


def slice_ids(me, size):
    mate = me ^ 1
    wrap = lambda v: v % size
    return jnp.stack(
        [me, mate, wrap(me + size - 2), wrap(me + 2), wrap(mate + size - 2), wrap(mate + 2),
         wrap(me + size - 4), wrap(mate + 4)]
    ).astype(jnp.int32)


def partial_kernel(ids, own_ref, mate_ref, *refs):
    count = len(refs) // 2
    part = own_ref.shape[1] // 2
    mine = ids[ids.shape[0] - 1]
    for k in range(count):
        w, out_ref = refs[k::count]
        unit = w.shape[1] // 3
        both = down = 0.0
        for half, rows in ((mine, own_ref), (1 - mine, mate_ref)):
            base = half * part
            at = pl.ds(pl.multiple_of(base, part), part)
            both += dot(rows[:, :part], w[at, : 2 * unit], ((1,), (0,)))
            for q in range(part // LANES):
                cots = rows[:, part + q * LANES : part + (q + 1) * LANES]
                at = pl.ds(pl.multiple_of(base + q * LANES, LANES), LANES)
                down += dot(cots, w[at, 2 * unit :], ((1,), (1,)))
        out_ref[...] = jnp.concatenate([both, down], axis=1).astype(BF)


def point_kernel(*refs):
    trio_ref, pair_ref = refs[-2:]
    total = refs[0][...].astype(F32)
    for part_ref in refs[1:-2]:
        total += part_ref[...].astype(F32)
    unit = total.shape[1] // 3
    gate, up, d_hidden = total[:, :unit], total[:, unit : 2 * unit], total[:, 2 * unit :]
    s = jax.nn.sigmoid(gate)
    hid = (gate * s * up).astype(BF)
    dg = (d_hidden * up * s * (1.0 + gate * (1.0 - s))).astype(BF)
    du = (d_hidden * gate * s).astype(BF)
    trio_ref[...] = jnp.concatenate([hid, dg, du], axis=1)
    pair_ref[...] = jnp.concatenate([dg, du], axis=1)


def share_kernel(which, ids, *refs):
    out_ref, acc = refs[-2:]
    count = len(refs) // 2 - 1
    part = out_ref.shape[1]
    mine = ids[ids.shape[0] - 1]
    at = pl.ds(pl.multiple_of((mine if which == 0 else 1 - mine) * part, part), part)
    for k in range(count):
        pair, w = refs[:-2][k::count]
        total = dot(pair[...], w[at, : pair.shape[1]], ((1,), (1,)))
        if k == 0:
            acc[...] = total
        else:
            acc[...] += total
    out_ref[...] = acc[...].astype(out_ref.dtype)


def grad_kernel(ids, *refs):
    rows = refs[:8]
    here, there, gg_ref, gu_ref, gd_ref = refs[8:]
    part = rows[0].shape[1] // 2
    trio = jnp.where(ids[8] != 0, there[...].astype(F32), here[...].astype(F32)).astype(BF)
    unit = trio.shape[1] // 3
    hid, dg, du = trio[:, :unit], trio[:, unit : 2 * unit], trio[:, 2 * unit :]
    for k in range(8):
        at = pl.ds(pl.multiple_of(ids[k] * part, part), part)
        gg_ref[at, :] = dot(rows[k][:, :part], dg, ((0,), (0,))).astype(BF)
        gu_ref[at, :] = dot(rows[k][:, :part], du, ((0,), (0,))).astype(BF)
        gd_ref[:, at] = dot(hid, rows[k][:, part:], ((0,), (0,))).astype(BF)


def call(kernel, scalars, args, outs, flops, scratch=()):
    vm = pl.BlockSpec(memory_space=pltpu.VMEM)
    size = lambda a: a.size * a.dtype.itemsize
    return pl.pallas_call(
        kernel,
        out_shape=outs,
        in_specs=[pl.BlockSpec(memory_space=pltpu.SMEM)] * len(scalars) + [vm] * len(args),
        out_specs=jax.tree.map(lambda _: vm, outs),
        scratch_shapes=list(scratch),
        compiler_params=pltpu.CompilerParams(vmem_limit_bytes=48 << 20),
        cost_estimate=pl.CostEstimate(
            flops=flops,
            bytes_accessed=sum(map(size, args)) + sum(map(size, jax.tree.leaves(outs))),
            transcendentals=0,
        ),
    )(*scalars, *args)


def shards(tokens, cotangent, w_gate, w_up, w_down, routes, gates, matching):
    n_tok, width = tokens.shape[2], tokens.shape[3]
    topk = routes.shape[3]
    experts, groups = lax.axis_size("expert"), lax.axis_size("dp")
    cap = 3 * groups * n_tok * topk // (2 * experts)
    low = cap - 1
    part = width // groups
    parts = part // LANES
    hidden = w_gate.shape[2]
    me_e, me_d = lax.axis_index("expert"), lax.axis_index("dp")
    expert_iota = jnp.arange(experts, dtype=jnp.int32)
    flipped = jnp.sum(jnp.where(expert_iota == me_e, matching, 0)) != me_e
    ids = jnp.concatenate([slice_ids(me_d, groups), flipped.astype(jnp.int32)[None]])
    across = lambda x: flip(x, "expert", experts // 2, experts)

    slot_count = experts * cap
    stride = -(-n_tok // 16) * 16
    lanes = 2 * part + LANES

    packed = call(
        pack_kernel, (), (tokens[0, 0], cotangent[0, 0], routes[0, 0], gates[0, 0]),
        jax.ShapeDtypeStruct((groups, stride, lanes), BF), 0,
    )
    column = lax.all_to_all(packed, "dp", split_axis=0, concat_axis=0, tiled=True)

    turns = (2, 6, 4)
    ring_len = groups // 2
    sources = jnp.stack([me_d // 2] + [(me_d ^ k) // 2 for k in turns] + [me_d % 2]).astype(jnp.int32)
    chunk = 2 * parts * low + 16 * (-(-2 * parts // 16))
    def route(rows):
        return call(
            functools.partial(route_kernel, n_tok, topk), (), (rows,),
            (
                jax.ShapeDtypeStruct((experts, chunk, LANES), BF),
                jax.ShapeDtypeStruct((groups * stride, slot_count), BF),
            ), 0,
        )

    to_home, places = route(column)

    cut = jax.ShapeDtypeStruct((2 * part, 3 * hidden), BF)
    near = after(sources, column)
    weights = (w_gate[0], w_up[0], w_down[0])
    far = lambda b, k: flip(b, "dp", k, groups)
    first = call(block_kernel, (near[1:3],), weights, (cut,) * 2, 0)
    middle = [far(b, k) for k, b in zip(turns, first)]
    rest = call(
        block_kernel, (after(near, *middle)[:: ring_len - 1],), weights, (cut,) * 2, SPAN_HINT
    )
    blocks = [rest[0], *middle, far(rest[1], turns[-1])]
    arrive = lambda sent: [sent[0]] + [far(b, k) for k, b in zip(turns, sent[1:])]

    def exchange(x):
        return lax.all_to_all(x, "expert", split_axis=0, concat_axis=0, tiled=True)

    arrived = exchange(to_home)
    both = from_chunks(after(arrived, *rest), experts, low, 2 * parts)
    mate_both = flip(both, "dp", 1, groups)
    unit = 2 * slot_count * width * hidden
    sums = call(
        partial_kernel, (sources,), (both, mate_both, *blocks),
        (jax.ShapeDtypeStruct((slot_count, 3 * hidden), BF),) * ring_len, 3 * unit,
    )
    sums = arrive(sums)
    trio, pair = call(
        point_kernel, (), sums,
        (
            jax.ShapeDtypeStruct((slot_count, 3 * hidden), BF),
            jax.ShapeDtypeStruct((slot_count, 2 * hidden), BF),
        ), unit // 100,
    )
    here, there = (both, mate_both), [across(after(v, mate_both)) for v in (both, mate_both)]
    pairs = arrive((pair,) * ring_len)
    pairs = lax.optimization_barrier((*pairs, there[0]))[:ring_len]
    slots = [jnp.where(flipped, a, b) for a, b in zip(there, here)]
    ring = gather_slices(after(slots[0], *pairs), slots[1], groups)

    halves = [
        call(
            functools.partial(share_kernel, which), (sources,), (*pairs, *blocks),
            jax.ShapeDtypeStruct((slot_count, part), kind), unit,
            [pltpu.VMEM((slot_count, part), F32)],
        )
        for which, kind in ((1, BF), (0, F32))
    ]
    share = (flip(halves[0], "dp", 1, groups).astype(F32) + halves[1]).astype(BF)
    share = after(share, there[1], ring[2], ring[3])
    shapes = tuple(jax.ShapeDtypeStruct(w.shape[1:], BF) for w in (w_gate, w_up, w_down))
    grads = call(grad_kernel, (ids,), (*ring, trio, across(trio)), shapes, 3 * unit)

    back = exchange(to_chunks(share, experts, low))
    back = from_chunks(after(back, ring[4], ring[5]), experts, low, parts)
    total = dot(places, back, ((1,), (0,))).astype(BF)
    mine = lax.all_to_all(total.reshape(groups, stride, part), "dp", split_axis=0, concat_axis=0, tiled=True)
    grad_input = mine[:, :n_tok].transpose(1, 0, 2).reshape(1, 1, n_tok, width)
    return grad_input, grads[0][None], grads[1][None], grads[2][None]


def solution(mesh):
    placed = (
        P("expert", "dp", None, None),
        P("expert", "dp", None, None),
        P("expert", None, "dp"),
        P("expert", None, "dp"),
        P("expert", "dp", None),
        P("expert", "dp", None, None),
        P("expert", "dp", None, None),
        P(),
    )
    return jax.shard_map(
        shards,
        mesh=mesh,
        in_specs=placed,
        out_specs=(
            P("expert", "dp", None, None),
            P("expert", None, "dp"),
            P("expert", None, "dp"),
            P("expert", "dp", None),
        ),
        check_vma=False,
    )
```

```python
import functools

import jax
import jax.numpy as jnp
from jax import lax
from jax.experimental import pallas as pl
from jax.experimental.pallas import tpu as pltpu
from jax.sharding import PartitionSpec as P

LANES = 128
BF = jnp.bfloat16
F32 = jnp.float32
SPAN_HINT = 14 * 10**9


def dot(a, b, dims):
    return lax.dot_general(a, b, (dims, ((), ())), preferred_element_type=F32)


def hop(x, axis, step, size):
    return lax.ppermute(x, axis, [(i, (i + step) % size) for i in range(size)])


def flip(x, axis, bit, size):
    return lax.ppermute(x, axis, [(i, i ^ bit) for i in range(size)])


def after(x, *others):
    return lax.optimization_barrier((x, *others))[0]


def pack_kernel(tok, cot, routes, gates, out):
    groups, rows, lanes = out.shape
    n_tok, topk = routes.shape
    part = (lanes - LANES) // 2
    lane = lax.broadcasted_iota(jnp.int32, (n_tok, LANES), 1)
    meta = jnp.zeros((n_tok, LANES), jnp.int32)
    for k in range(topk):
        g = gates[:, k : k + 1]
        for at, v in ((3 * k, routes[:, k : k + 1]), (3 * k + 1, g // 256), (3 * k + 2, g % 256)):
            meta = jnp.where(lane == at, v, meta)
    meta = meta.astype(F32).astype(BF)
    fill = jnp.zeros((rows - n_tok, lanes), BF)
    for d in range(groups):
        at = slice(d * part, (d + 1) * part)
        rows_here = jnp.concatenate([tok[:, at], cot[:, at], meta], axis=1)
        out[d] = jnp.concatenate([rows_here, fill], axis=0)


def block_kernel(ids, wg, wu, wd, *outs):
    span = outs[0].shape[0]
    unit = wg.shape[1]
    for k, out in enumerate(outs[: ids.shape[0]]):
        start = pl.multiple_of(ids[k] * span, span)
        out[:, :unit] = wg[pl.ds(start, span), :]
        out[:, unit : 2 * unit] = wu[pl.ds(start, span), :]
        down, base = (out, 2 * unit) if out.shape[1] > 2 * unit else (outs[-1], 0)
        for q in range(span // LANES):
            at = pl.ds(pl.multiple_of(start + q * LANES, LANES), LANES)
            down[q * LANES : (q + 1) * LANES, base : base + unit] = wd[:, at]


def route_kernel(n_tok, topk, rows_ref, out_ref, place_ref):
    groups, stride, lanes = rows_ref.shape
    experts, chunk, _ = out_ref.shape
    count = groups * stride
    cap = place_ref.shape[1] // experts
    low = cap - 1
    head = experts * low
    x = rows_ref[...].reshape(count, lanes)
    meta = x[:, lanes - LANES :].astype(F32)
    row = lax.broadcasted_iota(jnp.int32, (count, 1), 0)
    valid = row % stride < n_tok
    expert = lax.broadcasted_iota(jnp.int32, (count, experts), 1).astype(F32)
    named = [jnp.where(valid & (meta[:, 3 * k : 3 * k + 1] == expert), 1.0, 0.0) for k in range(topk)]
    every = sum(named)
    above = lax.broadcasted_iota(jnp.int32, (count, count), 0) > lax.broadcasted_iota(
        jnp.int32, (count, count), 1
    )
    earlier = dot(above.astype(F32).astype(BF), every.astype(BF), ((1,), (0,)))
    tail = chunk - low * (lanes - LANES) // LANES
    wide = lax.broadcasted_iota(jnp.int32, (count, head + experts * tail), 1)
    narrow = lax.broadcasted_iota(jnp.int32, (count, experts * cap), 1)
    pick = place = gate = None
    for k in range(topk):
        rank = jnp.sum(earlier * named[k], axis=1, keepdims=True).astype(jnp.int32)
        name = meta[:, 3 * k : 3 * k + 1].astype(jnp.int32)
        first = jnp.where(valid & (rank < low), name * low + rank, -1)
        last = jnp.where(valid & (rank >= low), name, -1)
        hit = (wide == first) | ((wide >= head) & ((wide - head) // tail == last))
        hit = jnp.where(hit, 1.0, 0.0).astype(BF)
        small = jnp.where((narrow == first) | ((narrow >= head) & (narrow - head == last)), 1.0, 0.0)
        g = dot(hit, x[:, lanes - LANES :], ((0,), (0,)))
        g = (g[:, 3 * k + 1 : 3 * k + 2] * 256.0 + g[:, 3 * k + 2 : 3 * k + 3]) * (1.0 / 65536.0)
        pick, place, gate = (hit, small, g) if k == 0 else (pick + hit, place + small, gate + g)
    place_ref[...] = place.astype(BF)
    parts = (lanes - LANES) // LANES
    slots = head + experts * tail
    spot = lax.broadcasted_iota(jnp.int32, (experts * tail, LANES), 0) % tail
    ends = jnp.zeros((experts * tail, LANES), F32)
    heads = []
    for q in range(parts):
        rows = dot(pick, x[:, q * LANES : (q + 1) * LANES], ((0,), (0,)))
        if q >= parts // 2:
            rows = rows * gate
        heads.append(rows[:head].reshape(experts, low, LANES))
        ends = jnp.where(spot == q, rows[head:], ends)
        if q % 2 == 1:
            pair = jnp.concatenate(heads, axis=1)
            out_ref[:, (q - 1) * low : (q + 1) * low, :] = pair.astype(BF)
            heads = []
    out_ref[:, parts * low :, :] = ends.reshape(experts, tail, LANES).astype(BF)


def to_chunks(x, experts, low):
    parts = x.shape[1] // LANES
    head = x[: experts * low].reshape(experts, low, parts, LANES)
    head = head.transpose(0, 2, 1, 3).reshape(experts, low * parts, LANES)
    last = x[experts * low :].reshape(experts, parts, LANES)
    pad = -(low + 1) * parts % 16
    return jnp.concatenate([head, last, jnp.zeros((experts, pad, LANES), x.dtype)], axis=1)


def from_chunks(y, experts, low, parts):
    head = y[:, : low * parts].reshape(experts, parts, low, LANES)
    head = head.transpose(0, 2, 1, 3).reshape(experts * low, parts * LANES)
    last = y[:, low * parts : (low + 1) * parts].reshape(experts, parts * LANES)
    return jnp.concatenate([head, last], axis=0)


def gather_slices(x, mate, size):
    own_up, own_down = hop(x, "dp", 2, size), hop(x, "dp", -2, size)
    mate_up, mate_down = hop(mate, "dp", 2, size), hop(mate, "dp", -2, size)
    own_far, mate_far = hop(own_up, "dp", 2, size), hop(mate_down, "dp", -2, size)
    return (x, mate, own_up, own_down, mate_up, mate_down, own_far, mate_far)


def slice_ids(me, size):
    mate = me ^ 1
    wrap = lambda v: v % size
    return jnp.stack(
        [me, mate, wrap(me + size - 2), wrap(me + 2), wrap(mate + size - 2), wrap(mate + 2),
         wrap(me + size - 4), wrap(mate + 4)]
    ).astype(jnp.int32)


def partial_kernel(ids, own_ref, mate_ref, *refs):
    count = len(refs) // 2
    blocks, last, outs = refs[:count], refs[count], refs[count + 1 :]
    part = own_ref.shape[1] // 2
    mine = ids[ids.shape[0] - 1]
    for k in range(count):
        w, out_ref = blocks[k], outs[k]
        unit = last.shape[1]
        wd, first = (w, 2 * unit) if w.shape[1] > 2 * unit else (last, 0)
        both = down = 0.0
        for half, rows in ((mine, own_ref), (1 - mine, mate_ref)):
            base = half * part
            at = pl.ds(pl.multiple_of(base, part), part)
            both += dot(rows[:, :part], w[at, : 2 * unit], ((1,), (0,)))
            for q in range(part // LANES):
                cots = rows[:, part + q * LANES : part + (q + 1) * LANES]
                at = pl.ds(pl.multiple_of(base + q * LANES, LANES), LANES)
                down += dot(cots, wd[at, first : first + unit], ((1,), (1,)))
        out_ref[...] = jnp.concatenate([both, down], axis=1).astype(BF)


def point_kernel(*refs):
    trio_ref, pair_ref = refs[-2:]
    total = refs[0][...].astype(F32)
    for part_ref in refs[1:-2]:
        total += part_ref[...].astype(F32)
    unit = total.shape[1] // 3
    gate, up, d_hidden = total[:, :unit], total[:, unit : 2 * unit], total[:, 2 * unit :]
    s = jax.nn.sigmoid(gate)
    hid = (gate * s * up).astype(BF)
    dg = (d_hidden * up * s * (1.0 + gate * (1.0 - s))).astype(BF)
    du = (d_hidden * gate * s).astype(BF)
    trio_ref[...] = jnp.concatenate([hid, dg, du], axis=1)
    pair_ref[...] = jnp.concatenate([dg, du], axis=1)


def share_kernel(which, ids, *refs):
    out_ref, acc = refs[-2:]
    count = len(refs) // 2 - 1
    part = out_ref.shape[1]
    mine = ids[ids.shape[0] - 1]
    at = pl.ds(pl.multiple_of((mine if which == 0 else 1 - mine) * part, part), part)
    for k in range(count):
        pair, w = refs[:-2][k::count]
        total = dot(pair[...], w[at, : pair.shape[1]], ((1,), (1,)))
        if k == 0:
            acc[...] = total
        else:
            acc[...] += total
    out_ref[...] = acc[...].astype(out_ref.dtype)


def grad_kernel(ids, *refs):
    rows = refs[:8]
    here, there, gg_ref, gu_ref, gd_ref = refs[8:]
    part = rows[0].shape[1] // 2
    trio = jnp.where(ids[8] != 0, there[...].astype(F32), here[...].astype(F32)).astype(BF)
    unit = trio.shape[1] // 3
    hid, dg, du = trio[:, :unit], trio[:, unit : 2 * unit], trio[:, 2 * unit :]
    for k in range(8):
        at = pl.ds(pl.multiple_of(ids[k] * part, part), part)
        gg_ref[at, :] = dot(rows[k][:, :part], dg, ((0,), (0,))).astype(BF)
        gu_ref[at, :] = dot(rows[k][:, :part], du, ((0,), (0,))).astype(BF)
        gd_ref[:, at] = dot(hid, rows[k][:, part:], ((0,), (0,))).astype(BF)


def call(kernel, scalars, args, outs, flops, scratch=()):
    vm = pl.BlockSpec(memory_space=pltpu.VMEM)
    size = lambda a: a.size * a.dtype.itemsize
    return pl.pallas_call(
        kernel,
        out_shape=outs,
        in_specs=[pl.BlockSpec(memory_space=pltpu.SMEM)] * len(scalars) + [vm] * len(args),
        out_specs=jax.tree.map(lambda _: vm, outs),
        scratch_shapes=list(scratch),
        compiler_params=pltpu.CompilerParams(vmem_limit_bytes=48 << 20),
        cost_estimate=pl.CostEstimate(
            flops=flops,
            bytes_accessed=sum(map(size, args)) + sum(map(size, jax.tree.leaves(outs))),
            transcendentals=0,
        ),
    )(*scalars, *args)


def shards(tokens, cotangent, w_gate, w_up, w_down, routes, gates, matching):
    n_tok, width = tokens.shape[2], tokens.shape[3]
    topk = routes.shape[3]
    experts, groups = lax.axis_size("expert"), lax.axis_size("dp")
    cap = 3 * groups * n_tok * topk // (2 * experts)
    low = cap - 1
    part = width // groups
    parts = part // LANES
    hidden = w_gate.shape[2]
    me_e, me_d = lax.axis_index("expert"), lax.axis_index("dp")
    expert_iota = jnp.arange(experts, dtype=jnp.int32)
    flipped = jnp.sum(jnp.where(expert_iota == me_e, matching, 0)) != me_e
    ids = jnp.concatenate([slice_ids(me_d, groups), flipped.astype(jnp.int32)[None]])
    across = lambda x: flip(x, "expert", experts // 2, experts)

    slot_count = experts * cap
    stride = -(-n_tok // 16) * 16
    lanes = 2 * part + LANES

    packed = call(
        pack_kernel, (), (tokens[0, 0], cotangent[0, 0], routes[0, 0], gates[0, 0]),
        jax.ShapeDtypeStruct((groups, stride, lanes), BF), 0,
    )
    column = lax.all_to_all(packed, "dp", split_axis=0, concat_axis=0, tiled=True)

    turns = (2, 6, 4)
    ring_len = groups // 2
    sources = jnp.stack([me_d // 2] + [(me_d ^ k) // 2 for k in turns] + [me_d % 2]).astype(jnp.int32)
    chunk = 2 * parts * low + 16 * (-(-2 * parts // 16))
    def route(rows):
        return call(
            functools.partial(route_kernel, n_tok, topk), (), (rows,),
            (
                jax.ShapeDtypeStruct((experts, chunk, LANES), BF),
                jax.ShapeDtypeStruct((groups * stride, slot_count), BF),
            ), 0,
        )

    to_home, places = route(column)

    cut = jax.ShapeDtypeStruct((2 * part, 3 * hidden), BF)
    near = after(sources, column)
    weights = (w_gate[0], w_up[0], w_down[0])
    far = lambda b, k: flip(b, "dp", k, groups)
    first = call(block_kernel, (near[1:3],), weights, (cut,) * 2, 0)
    middle = [far(b, k) for k, b in zip(turns, first)]
    rest = call(
        block_kernel, (after(near, *middle)[:: ring_len - 1],), weights,
        (cut, *(jax.ShapeDtypeStruct((2 * part, n * hidden), BF) for n in (2, 1))), SPAN_HINT,
    )
    blocks = [rest[0], *middle, far(rest[1], turns[-1])]
    last = far(rest[2], turns[-1])
    arrive = lambda sent: [sent[0]] + [far(b, k) for k, b in zip(turns, sent[1:])]

    def exchange(x):
        return lax.all_to_all(x, "expert", split_axis=0, concat_axis=0, tiled=True)

    arrived = exchange(to_home)
    both = from_chunks(after(arrived, last, *rest), experts, low, 2 * parts)
    mate_both = flip(both, "dp", 1, groups)
    unit = 2 * slot_count * width * hidden
    sums = call(
        partial_kernel, (sources,), (both, mate_both, *blocks, last),
        (jax.ShapeDtypeStruct((slot_count, 3 * hidden), BF),) * ring_len, 3 * unit,
    )
    sums = arrive(sums)
    trio, pair = call(
        point_kernel, (), sums,
        (
            jax.ShapeDtypeStruct((slot_count, 3 * hidden), BF),
            jax.ShapeDtypeStruct((slot_count, 2 * hidden), BF),
        ), unit // 100,
    )
    here, there = (both, mate_both), [across(after(v, mate_both)) for v in (both, mate_both)]
    pairs = arrive((pair,) * ring_len)
    pairs = lax.optimization_barrier((*pairs, there[0]))[:ring_len]
    slots = [jnp.where(flipped, a, b) for a, b in zip(there, here)]
    ring = gather_slices(after(slots[0], *pairs), slots[1], groups)

    halves = [
        call(
            functools.partial(share_kernel, which), (sources,), (*pairs, *blocks),
            jax.ShapeDtypeStruct((slot_count, part), kind), unit,
            [pltpu.VMEM((slot_count, part), F32)],
        )
        for which, kind in ((1, BF), (0, F32))
    ]
    share = (flip(halves[0], "dp", 1, groups).astype(F32) + halves[1]).astype(BF)
    share = after(share, there[1], ring[2], ring[3])
    shapes = tuple(jax.ShapeDtypeStruct(w.shape[1:], BF) for w in (w_gate, w_up, w_down))
    grads = call(grad_kernel, (ids,), (*ring, trio, across(trio)), shapes, 3 * unit)

    back = exchange(to_chunks(share, experts, low))
    back = from_chunks(after(back, ring[4], ring[5]), experts, low, parts)
    total = dot(places, back, ((1,), (0,))).astype(BF)
    mine = lax.all_to_all(total.reshape(groups, stride, part), "dp", split_axis=0, concat_axis=0, tiled=True)
    grad_input = mine[:, :n_tok].transpose(1, 0, 2).reshape(1, 1, n_tok, width)
    return grad_input, grads[0][None], grads[1][None], grads[2][None]


def solution(mesh):
    placed = (
        P("expert", "dp", None, None),
        P("expert", "dp", None, None),
        P("expert", None, "dp"),
        P("expert", None, "dp"),
        P("expert", "dp", None),
        P("expert", "dp", None, None),
        P("expert", "dp", None, None),
        P(),
    )
    return jax.shard_map(
        shards,
        mesh=mesh,
        in_specs=placed,
        out_specs=(
            P("expert", "dp", None, None),
            P("expert", None, "dp"),
            P("expert", None, "dp"),
            P("expert", "dp", None),
        ),
        check_vma=False,
    )
```
